32 devices in a mesh: seq: 8 (over y, x, core), mp: 4 (over z).
Axes of the slice: x: 2, y: 2, z: 4, core: 2. Of those that a mesh axis runs over, the one named last changes fastest.
Arguments:
- byte_states: bfloat16 [4096, 1024], P('seq'), may hold values from -6 to 6
- patch_starts: int32 [8, 192], P('seq'), may hold values from 0 to 512, as said below
- patch_counts: int32 [8, 1], P('seq'), may hold values from 64 to 192, as said below
- patch_owner: int32 [8, 192], P('seq'), may hold values from -1 to 7, as said below
- enc_query: bfloat16 [1024, 1024], P(None, 'mp'), may hold values from -0.1875 to 0.1875
- enc_key: bfloat16 [1024, 1024], P(None, 'mp'), may hold values from -0.1875 to 0.1875
- enc_value: bfloat16 [1024, 1024], P(None, 'mp'), may hold values from -0.1875 to 0.1875
- enc_out: bfloat16 [1024, 4096], P('mp'), may hold values from -0.1875 to 0.1875
- up_proj: bfloat16 [4096, 7168], P('seq', 'mp'), may hold values from -0.09375 to 0.09375
- down_proj: bfloat16 [4096, 7168], P('seq', 'mp'), may hold values from -0.0625 to 0.0625
- dec_query: bfloat16 [1024, 1024], P(None, 'mp'), may hold values from -0.1875 to 0.1875
- dec_key: bfloat16 [4096, 1024], P(None, 'mp'), may hold values from -0.09375 to 0.09375
- dec_value: bfloat16 [4096, 1024], P(None, 'mp'), may hold values from -0.09375 to 0.09375
- dec_out: bfloat16 [1024, 1024], P('mp'), may hold values from -0.1875 to 0.1875
- latent_cotangent: bfloat16 [1536, 4096], P('seq', 'mp'), may hold values from -6 to 6
Outputs:
- decoded: bfloat16 [4096, 1024], P('seq', 'mp')
- patch_grad: bfloat16 [1536, 4096], P('seq', 'mp')
- down_grad: bfloat16 [4096, 7168], P('seq', 'mp')
The draws below stay inside these ranges and needn't reach their ends.
Inputs may be any that keep to these rules, and one draw needn't show every extreme that they name: `patch_counts`: the counts of all shards sum to 128 times the number of shards; some shard has exactly 192 patches and some exactly 64. `patch_starts`: in each shard's row the first entry is 0, the first count entries rise strictly and stay below 512, and the remaining entries equal 512. `patch_owner`: entries at or beyond the shard's count are -1, the others name a latent shard. Every latent shard owns exactly 128 patches in all and at most 24 of one byte shard's patches; a shard with 192 patches gives exactly 24 to every latent shard.
All inputs are finite; a program needn't handle non-finite values.
Results may differ from the reference program's by a relative error of at most 0.024.
Values may be sent and summed in bfloat16 or wider, within the bound.
No kernel may reach another device: no remote copies, remote signals or barrier semaphores. Data moves between devices by JAX's collectives and lax.ppermute only.
A program may use at most 128 MiB of HBM per device.

```python
import math
import jax
import jax.numpy as jnp
from jax import lax

D = 4096
DL = 1024
HL = 16
FF = 7168
CAP = 128
PMAX = 192
BYTE_DEV = 512
BYTES = 4096
N_SEQ = 8
N_MP = 4


def patch_plan(key):
    base_key = jax.random.fold_in(key, 9173)
    pair_key, extra_key, cut_key, shuffle_key = jax.random.split(base_key, 4)
    pairing = jax.random.permutation(pair_key, N_SEQ)
    extras = jax.random.randint(extra_key, (N_SEQ // 2,), 0, CAP // 2 + 1).astype(jnp.int32)
    extras = extras.at[0].set(CAP // 2)
    totals = jnp.zeros((N_SEQ,), jnp.int32)
    totals = totals.at[pairing[0::2]].set(CAP + extras)
    totals = totals.at[pairing[1::2]].set(CAP - extras)
    cut_keys = jax.random.split(cut_key, N_SEQ)
    ranks = jax.vmap(lambda single: jax.random.permutation(single, BYTE_DEV - 1))(cut_keys).astype(jnp.int32)
    chosen = ranks < totals[:, None] - 1
    marks = jnp.where(chosen, jnp.arange(1, BYTE_DEV, dtype=jnp.int32)[None, :], BYTE_DEV)
    marks = jnp.concatenate([jnp.zeros((N_SEQ, 1), jnp.int32), marks], axis=1)
    starts_all = jnp.sort(marks, axis=1)[:, :PMAX]
    offsets = jnp.cumsum(totals) - totals
    slot_ids = jnp.arange(PMAX, dtype=jnp.int32)
    dealt = (offsets[:, None] + slot_ids[None, :]) % N_SEQ
    is_live = slot_ids[None, :] < totals[:, None]
    shuffle_keys = jax.random.split(shuffle_key, N_SEQ)
    shuffled = jax.vmap(lambda single: jax.random.permutation(single, PMAX))(shuffle_keys).astype(jnp.int32)
    sort_key = jnp.where(is_live, shuffled, PMAX + slot_ids[None, :])
    ordering = jnp.argsort(sort_key, axis=1, stable=True)
    owners = jnp.take_along_axis(dealt, ordering, axis=1)
    owners = jnp.where(is_live, owners, -1).astype(jnp.int32)
    return (totals, starts_all.astype(jnp.int32), owners)


def draw_patch_counts(key, part):
    return patch_plan(key)[0][:, None].astype(jnp.int32)


def draw_patch_starts(key, part):
    return patch_plan(key)[1]


def draw_patch_owner(key, part):
    return patch_plan(key)[2]


def shard_levels(key, shape, cuts, smallest, top_value):
    def one(axis_at, parts):
        draws = jax.random.uniform(jax.random.fold_in(jax.random.fold_in(key, 6), axis_at), (parts,), jnp.float32, smallest / len(cuts), top_value / len(cuts))
        return jnp.repeat(jnp.exp(draws), shape[axis_at] // parts).reshape((-1,) + (1,) * (len(shape) - axis_at - 1))

    level = one(*cuts[0])
    for cut in cuts[1:]:
        level = level * one(*cut)
    return level


def noise(own_key, extent, scale, bound, pieces=(), kind=jnp.bfloat16):
    gain = shard_levels(own_key, extent, pieces, -0.22, 0.18) if pieces else 1.0
    values = jax.random.normal(own_key, extent, jnp.float32) * scale * gain
    return jnp.minimum(jnp.maximum(values, -bound), bound).astype(kind)


def setup_inputs(seed: int = 0) -> dict:
    seeds = jax.random.split(jax.random.key(seed), 16)
    return {
        "byte_states": noise(seeds[0], (BYTES, DL), 1.0, 6.0, ((0, 8),)),
        "patch_starts": draw_patch_starts(jax.random.fold_in(seeds[15], 71), 0),
        "patch_counts": draw_patch_counts(jax.random.fold_in(seeds[15], 71), 0),
        "patch_owner": draw_patch_owner(jax.random.fold_in(seeds[15], 71), 0),
        "enc_query": noise(seeds[4], (DL, DL), DL ** -0.5, 0.1875, ((1, 4),)),
        "enc_key": noise(seeds[5], (DL, DL), DL ** -0.5, 0.1875, ((1, 4),)),
        "enc_value": noise(seeds[6], (DL, DL), DL ** -0.5, 0.1875, ((1, 4),)),
        "enc_out": noise(seeds[7], (DL, D), DL ** -0.5, 0.1875, ((0, 4),)),
        "up_proj": noise(seeds[8], (D, FF), D ** -0.5, 0.09375, ((0, 8), (1, 4))),
        "down_proj": noise(seeds[9], (D, FF), FF ** -0.5, 0.0625, ((0, 8), (1, 4))),
        "dec_query": noise(seeds[10], (DL, DL), DL ** -0.5, 0.1875, ((1, 4),)),
        "dec_key": noise(seeds[11], (D, DL), D ** -0.5, 0.09375, ((1, 4),)),
        "dec_value": noise(seeds[12], (D, DL), D ** -0.5, 0.09375, ((1, 4),)),
        "dec_out": noise(seeds[13], (DL, DL), DL ** -0.5, 0.1875, ((0, 4),)),
        "latent_cotangent": noise(seeds[14], (N_SEQ * PMAX, D), 1.0, 6.0, ((0, 8), (1, 4))),
    }


MASKED = -1e+30

def gelu_back(hidden_pre, incoming):
    return jax.vjp(jax.nn.gelu, hidden_pre)[1](incoming)[0]

def attend(queries, keys_in, values_in, allowed, head_count):
    row_count = queries.shape[0]
    col_count = keys_in.shape[0]
    head_width = queries.shape[1] // head_count
    query_heads = queries.astype(jnp.float32).reshape(row_count, head_count, head_width)
    key_heads = keys_in.astype(jnp.float32).reshape(col_count, head_count, head_width)
    value_heads = values_in.astype(jnp.float32).reshape(col_count, head_count, head_width)
    scores = jnp.einsum('rhd,chd->hrc', query_heads, key_heads) / head_width ** 0.5
    scores = jnp.where(allowed[None], scores, MASKED)
    weights = jax.nn.softmax(scores, axis=-1).astype(jnp.bfloat16)
    mixed = jnp.einsum('hrc,chd->rhd', weights.astype(jnp.float32), value_heads)
    return mixed.reshape(row_count, head_count * head_width).astype(jnp.bfloat16)

def grouped_right(right):
    inner_count = right.shape[0]
    return right.astype(jnp.float32).reshape(N_MP, inner_count // N_MP, right.shape[1])

def grouped_apply(left, prepared):
    row_count = left.shape[0]
    left_groups = left.astype(jnp.float32).reshape(row_count, N_MP, prepared.shape[1])
    partials = jnp.einsum('rgk,gkm->grm', left_groups, prepared).astype(jnp.bfloat16)
    return lax.optimization_barrier(jnp.sum(partials.astype(jnp.float32), axis=0))

def encode(states, patch_start, patch_total, enc_query, enc_key, enc_value, enc_ready):
    patch_end = jnp.concatenate([patch_start[1:], jnp.full((1,), BYTE_DEV, jnp.int32)])
    positions = jnp.arange(BYTE_DEV, dtype=jnp.int32)
    member = (positions[None, :] >= patch_start[:, None]) & (positions[None, :] < patch_end[:, None])
    lengths = lax.optimization_barrier(jnp.sum(member.astype(jnp.float32), axis=1))
    pooled = jnp.dot(member.astype(jnp.bfloat16), states, preferred_element_type=jnp.float32)
    pooled = (pooled / jnp.maximum(lengths, 1.0)[:, None]).astype(jnp.bfloat16)
    queries = jnp.dot(pooled, enc_query, preferred_element_type=jnp.float32).astype(jnp.bfloat16)
    keys_in = jnp.dot(states, enc_key, preferred_element_type=jnp.float32).astype(jnp.bfloat16)
    values_in = jnp.dot(states, enc_value, preferred_element_type=jnp.float32).astype(jnp.bfloat16)
    mixed = attend(queries, keys_in, values_in, member, HL)
    summed = grouped_apply(mixed, enc_ready)
    is_valid = jnp.arange(PMAX, dtype=jnp.int32) < patch_total
    return jnp.where(is_valid[:, None], summed, 0.0).astype(jnp.bfloat16)

def decode(states, patch_start, latents, dec_query, dec_key, dec_value, dec_ready):
    positions = jnp.arange(BYTE_DEV, dtype=jnp.int32)
    home_patch = lax.optimization_barrier(jnp.sum((patch_start[None, :] <= positions[:, None]).astype(jnp.int32), axis=1)) - 1
    allowed = jnp.arange(PMAX, dtype=jnp.int32)[None, :] <= home_patch[:, None]
    queries = jnp.dot(states, dec_query, preferred_element_type=jnp.float32).astype(jnp.bfloat16)
    keys_in = jnp.dot(latents, dec_key, preferred_element_type=jnp.float32).astype(jnp.bfloat16)
    values_in = jnp.dot(latents, dec_value, preferred_element_type=jnp.float32).astype(jnp.bfloat16)
    mixed = attend(queries, keys_in, values_in, allowed, HL)
    return (states.astype(jnp.float32) + grouped_apply(mixed, dec_ready)).astype(jnp.bfloat16)

def reference(byte_states, patch_starts, patch_counts, patch_owner, enc_query, enc_key, enc_value, enc_out, up_proj, down_proj, dec_query, dec_key, dec_value, dec_out, latent_cotangent):
    states_all = byte_states.reshape(N_SEQ, BYTE_DEV, DL)
    enc_ready = grouped_right(enc_out)

    def shard_encode(bundle):
        return encode(bundle[0], bundle[1], bundle[2], enc_query, enc_key, enc_value, enc_ready)
    patches = lax.map(shard_encode, (states_all, patch_starts, patch_counts[:, 0]))
    slot_total = N_SEQ * PMAX
    patches_flat = patches.reshape(slot_total, D)
    owner_flat = patch_owner.reshape(-1)
    flat_index = jnp.arange(slot_total, dtype=jnp.int32)
    sort_key = jnp.where(owner_flat >= 0, owner_flat * slot_total + flat_index, N_SEQ * slot_total + flat_index)
    routed = jnp.argsort(sort_key)[:N_SEQ * CAP].astype(jnp.int32)
    rows_grouped = patches_flat[routed].reshape(N_SEQ, CAP, D)
    grads_grouped = latent_cotangent[routed].reshape(N_SEQ, CAP, D)
    down_ready = grouped_right(down_proj.T)
    up_ready = grouped_right(up_proj.T)

    def latent_group(running, bundle):
        rows_in, grads_in = bundle
        hidden_pre = jnp.dot(rows_in, up_proj, preferred_element_type=jnp.float32)
        hidden = jax.nn.gelu(hidden_pre).astype(jnp.bfloat16)
        latent_rows = (rows_in.astype(jnp.float32) + grouped_apply(hidden, down_ready)).astype(jnp.bfloat16)
        backward = jnp.dot(grads_in, down_proj, preferred_element_type=jnp.float32)
        inner = gelu_back(hidden_pre, backward).astype(jnp.bfloat16)
        grad_rows = (grads_in.astype(jnp.float32) + grouped_apply(inner, up_ready)).astype(jnp.bfloat16)
        grad_term = jnp.dot(grads_in.T, hidden, preferred_element_type=jnp.float32).astype(jnp.bfloat16)
        return (running + grad_term.astype(jnp.float32), (latent_rows, grad_rows))
    running, outputs = lax.scan(latent_group, jnp.zeros((D, FF), jnp.float32), (rows_grouped, grads_grouped))
    latent_flat = jnp.zeros((slot_total, D), jnp.bfloat16).at[routed].set(outputs[0].reshape(-1, D))
    patch_grad = jnp.zeros((slot_total, D), jnp.bfloat16).at[routed].set(outputs[1].reshape(-1, D))
    down_grad = (running * (1.0 / math.sqrt(N_SEQ * CAP))).astype(jnp.bfloat16)
    dec_ready = grouped_right(dec_out)

    def shard_decode(bundle):
        return decode(bundle[0], bundle[1], bundle[2], dec_query, dec_key, dec_value, dec_ready)
    decoded = lax.map(shard_decode, (states_all, patch_starts, latent_flat.reshape(N_SEQ, PMAX, D)))
    return (decoded.reshape(N_SEQ * BYTE_DEV, DL), patch_grad, down_grad)
```

```python
import math

import jax
import jax.numpy as jnp
from jax import lax
from jax.sharding import PartitionSpec as P

HD = 64
CAP = 128
MASKED = -1e30


BF = jnp.bfloat16
F32 = jnp.float32


def gelu_back(hidden_pre, incoming):
    return jax.vjp(jax.nn.gelu, hidden_pre)[1](incoming)[0]


def attend(queries, keys_in, values_in, allowed, head_count):
    row_count = queries.shape[0]
    col_count = keys_in.shape[0]
    head_width = queries.shape[1] // head_count
    query_heads = queries.reshape(row_count, head_count, head_width)
    key_heads = keys_in.reshape(col_count, head_count, head_width)
    value_heads = values_in.reshape(col_count, head_count, head_width)
    scores = (
        jnp.einsum("rhd,chd->hrc", query_heads, key_heads, preferred_element_type=F32)
        / head_width**0.5
    )
    scores = jnp.where(allowed[None], scores, MASKED)
    weights = jax.nn.softmax(scores, axis=-1).astype(BF)
    mixed = jnp.einsum("hrc,chd->rhd", weights, value_heads, preferred_element_type=F32)
    return mixed.reshape(row_count, head_count * head_width).astype(BF)


def dot(left, right):
    return jnp.dot(left, right, preferred_element_type=F32)


def contract_last(left, right):
    return lax.dot_general(left, right, (((1,), (1,)), ((), ())), preferred_element_type=F32)


def contract_first(left, right):
    return lax.dot_general(left, right, (((0,), (0,)), ((), ())), preferred_element_type=F32)


def seq_swap(value, bits):
    return lax.ppermute(value, "seq", [(i, i ^ bits) for i in range(lax.axis_size("seq"))])


def mp_swap(value, bits):
    return lax.ppermute(value, "mp", [(i, i ^ bits) for i in range(lax.axis_size("mp"))])


def gather_mp(value):
    return [value] + [mp_swap(value, k) for k in range(1, lax.axis_size("mp"))]


def exchange_mp(pieces):
    return [pieces[0]] + [mp_swap(pieces[k], k) for k in range(1, len(pieces))]


def gather_seq(value):
    chips = lax.axis_size("seq") // 2
    same = jnp.stack([value] + [seq_swap(value, 2 * i) for i in range(1, chips)])
    other = seq_swap(same, 1)
    return jnp.stack([same, other], axis=1)


def exchange_seq(blocks):
    chips = blocks.shape[0]
    mine = blocks[:, 0]
    swapped = seq_swap(blocks[:, 1], 1)
    pair = jnp.stack([mine, swapped], axis=1)
    return jnp.stack([pair[0]] + [seq_swap(pair[i], 2 * i) for i in range(1, chips)])


def scatter_sum_seq(partial):
    size = lax.axis_size("seq")
    chips = size // 2
    blocks = partial.reshape(chips, 2, partial.shape[0] // size, partial.shape[1])
    arrived = seq_swap(blocks[:, 1].astype(BF), 1)
    summed = blocks[:, 0] + arrived.astype(F32)
    total = summed[0]
    sent = [seq_swap(summed[i].astype(BF), 2 * i) for i in range(1, chips)]
    for piece in sent:
        total = total + piece.astype(F32)
    return total


def per_device(
    byte_states,
    patch_starts,
    patch_counts,
    patch_owner,
    enc_query,
    enc_key,
    enc_value,
    enc_out,
    up_proj,
    down_proj,
    dec_query,
    dec_key,
    dec_value,
    dec_out,
    latent_cotangent,
):
    groups = lax.axis_size("seq")
    chips = groups // 2
    lanes = lax.axis_size("mp")
    here = lax.axis_index("seq")
    lane_index = lax.axis_index("mp")
    byte_count = byte_states.shape[0]
    slots = patch_starts.shape[1]
    total_rows = groups * CAP
    slice_width = up_proj.shape[0]
    sub = slice_width // lanes
    per_lane = groups // lanes
    patch_start = patch_starts[0]
    patch_total = patch_counts[0, 0]

    cot_blocks = latent_cotangent.reshape(slots, per_lane, lanes, sub)
    cot_blocks = jnp.transpose(cot_blocks, (2, 0, 1, 3))
    cot_pieces = [
        lax.dynamic_index_in_dim(cot_blocks, lane_index ^ k, 0, keepdims=False)
        for k in range(lanes)
    ]
    cot_got = exchange_mp(cot_pieces)
    by_slice = jnp.zeros((lanes, per_lane, slots, sub), BF)
    for k in range(lanes):
        by_slice = lax.dynamic_update_slice_in_dim(
            by_slice, jnp.transpose(cot_got[k], (1, 0, 2))[None], lane_index ^ k, 0
        )
    by_slice = by_slice.reshape(groups, slots, sub)
    relative = jnp.arange(groups, dtype=jnp.int32) ^ here
    by_slice = jnp.take(by_slice, relative, axis=0)
    tail = jnp.full((groups, 16, sub), patch_total.astype(F32)).astype(BF)
    cot_sent = jnp.concatenate([by_slice, tail], axis=1)
    cot_here = exchange_seq(cot_sent.reshape(chips, 2, slots + 16, sub)).reshape(
        groups, slots + 16, sub
    )
    counts = cot_here[:, slots, 0].astype(F32).astype(jnp.int32)
    cot_slots = cot_here[:, :slots].reshape(groups * slots, sub)

    before = relative[None, :] < relative[:, None]
    offsets = jnp.sum(jnp.where(before, counts[None, :], 0), axis=1)
    slot_ids = jnp.arange(slots, dtype=jnp.int32)
    places = jnp.where(slot_ids[None, :] < counts[:, None], offsets[:, None] + slot_ids[None, :], -1)
    places = places.reshape(groups * slots)
    row_ids = (relative[:, None] * CAP + jnp.arange(CAP, dtype=jnp.int32)[None, :]).reshape(
        total_rows
    )
    selector = (row_ids[:, None] == places[None, :]).astype(BF)

    cot_packed = dot(selector, cot_slots).astype(BF)
    cot_all = gather_mp(cot_packed)
    cot_slice = jnp.zeros((total_rows, slice_width), BF)
    for k in range(lanes):
        cot_slice = lax.dynamic_update_slice_in_dim(
            cot_slice, cot_all[k], (lane_index ^ k) * sub, 1
        )

    enc_own = lax.dynamic_slice_in_dim(enc_out, here * slice_width, slice_width, 1)
    enc_slice = jnp.concatenate(gather_mp(enc_own), axis=0)

    patch_end = jnp.concatenate([patch_start[1:], jnp.full((1,), byte_count, jnp.int32)])
    positions = jnp.arange(byte_count, dtype=jnp.int32)
    member = (positions[None, :] >= patch_start[:, None]) & (
        positions[None, :] < patch_end[:, None]
    )
    lengths = jnp.sum(member.astype(F32), axis=1)
    pooled = dot(member.astype(BF), byte_states)
    pooled = (pooled / jnp.maximum(lengths, 1.0)[:, None]).astype(BF)
    queries = dot(pooled, enc_query).astype(BF)
    keys_in = dot(byte_states, enc_key).astype(BF)
    values_in = dot(byte_states, enc_value).astype(BF)
    mixed = attend(queries, keys_in, values_in, member, enc_query.shape[1] // HD)
    mixed = jnp.concatenate(gather_mp(mixed), axis=1)
    mixed_all = gather_seq(mixed).reshape(groups * slots, mixed.shape[1])
    rows_slots = dot(mixed_all, enc_slice).astype(BF)
    rows = dot(selector, rows_slots).astype(BF)

    hidden_pre = scatter_sum_seq(dot(rows, up_proj))
    hidden = jax.nn.gelu(hidden_pre).astype(BF)
    hidden_all = gather_seq(hidden).reshape(total_rows, hidden.shape[1])
    forward_part = contract_last(hidden_all, down_proj).astype(BF)

    backward = scatter_sum_seq(dot(cot_slice, down_proj))
    inner = gelu_back(hidden_pre, backward).astype(BF)
    inner_all = gather_seq(inner).reshape(total_rows, inner.shape[1])
    backward_part = contract_last(inner_all, up_proj).astype(BF)
    down_grad = (
        contract_first(cot_slice, hidden_all) * (1.0 / math.sqrt(total_rows))
    ).astype(BF)

    def sum_lanes(part):
        got = exchange_mp(
            [
                lax.dynamic_slice_in_dim(part, (lane_index ^ k) * sub, sub, 1)
                for k in range(lanes)
            ]
        )
        total = got[0].astype(F32)
        for piece in got[1:]:
            total = total + piece.astype(F32)
        return total

    def send_home(packed):
        home = contract_first(selector, packed).astype(BF)
        return exchange_seq(home.reshape(chips, 2, slots, sub)).reshape(groups, slots, sub)

    rows_own = lax.dynamic_slice_in_dim(rows, lane_index * sub, sub, 1)
    latent_rows = (rows_own.astype(F32) + sum_lanes(forward_part)).astype(BF)
    latent_here = send_home(latent_rows)
    latent_lanes = gather_mp(latent_here)

    order = (
        relative[None, :] * lanes + (jnp.arange(lanes, dtype=jnp.int32) ^ lane_index)[:, None]
    ).reshape(-1)
    key_blocks = jnp.take(dec_key.reshape(groups * lanes, sub, -1), order, axis=0)
    value_blocks = jnp.take(dec_value.reshape(groups * lanes, sub, -1), order, axis=0)
    latent_full = jnp.stack(latent_lanes).reshape(lanes * groups, slots, sub)
    latent_full = jnp.transpose(latent_full, (1, 0, 2)).reshape(slots, -1)
    dec_keys = dot(latent_full, key_blocks.reshape(dec_key.shape)).astype(BF)
    dec_values = dot(latent_full, value_blocks.reshape(dec_value.shape)).astype(BF)
    home_patch = jnp.sum((patch_start[None, :] <= positions[:, None]).astype(jnp.int32), axis=1) - 1
    allowed = slot_ids[None, :] <= home_patch[:, None]
    dec_queries = dot(byte_states, dec_query).astype(BF)
    byte_mixed = attend(dec_queries, dec_keys, dec_values, allowed, dec_query.shape[1] // HD)
    decoded_part = dot(byte_mixed, dec_out).astype(BF)
    width_here = decoded_part.shape[1] // lanes
    got = exchange_mp(
        [
            lax.dynamic_slice_in_dim(decoded_part, (lane_index ^ k) * width_here, width_here, 1)
            for k in range(lanes)
        ]
    )
    own_cols = lax.dynamic_slice_in_dim(byte_states, lane_index * width_here, width_here, 1)
    decoded = own_cols.astype(F32)
    for piece in got:
        decoded = decoded + piece.astype(F32)
    decoded = decoded.astype(BF)

    grad_here = send_home(sum_lanes(backward_part).astype(BF))
    grad_abs = jnp.take(grad_here, relative, axis=0).reshape(lanes, per_lane, slots, sub)
    grad_got = exchange_mp(
        [
            lax.dynamic_index_in_dim(grad_abs, lane_index ^ k, 0, keepdims=False)
            for k in range(lanes)
        ]
    )
    grad_cols = jnp.zeros((lanes, per_lane, slots, sub), BF)
    for k in range(lanes):
        grad_cols = lax.dynamic_update_slice_in_dim(
            grad_cols, grad_got[k][None], lane_index ^ k, 0
        )
    grad_cols = jnp.transpose(grad_cols, (2, 1, 0, 3)).reshape(slots, -1)
    live = patch_owner[0] >= 0
    patch_grad = latent_cotangent.astype(F32) + grad_cols.astype(F32)
    patch_grad = jnp.where(live[:, None], patch_grad, 0.0).astype(BF)
    return (decoded, patch_grad, down_grad)


def solution(mesh):
    return jax.shard_map(
        per_device,
        mesh=mesh,
        in_specs=(
            P("seq", None),
            P("seq", None),
            P("seq", None),
            P("seq", None),
            P(None, "mp"),
            P(None, "mp"),
            P(None, "mp"),
            P("mp", None),
            P("seq", "mp"),
            P("seq", "mp"),
            P(None, "mp"),
            P(None, "mp"),
            P(None, "mp"),
            P("mp", None),
            P("seq", "mp"),
        ),
        out_specs=(P("seq", "mp"), P("seq", "mp"), P("seq", "mp")),
        check_vma=False,
    )
```

```python
import math

import jax
import jax.numpy as jnp
from jax import lax
from jax.experimental import pallas as pl
from jax.experimental.pallas import tpu as pltpu
from jax.sharding import PartitionSpec as P

HD = 64
CAP = 128
MASKED = -1e30


BF = jnp.bfloat16
F32 = jnp.float32


def gelu_back(hidden_pre, incoming):
    return jax.vjp(jax.nn.gelu, hidden_pre)[1](incoming)[0]


def attend(queries, keys_in, values_in, allowed, head_count):
    row_count = queries.shape[0]
    col_count = keys_in.shape[0]
    head_width = queries.shape[1] // head_count
    query_heads = queries.reshape(row_count, head_count, head_width)
    key_heads = keys_in.reshape(col_count, head_count, head_width)
    value_heads = values_in.reshape(col_count, head_count, head_width)
    scores = (
        jnp.einsum("rhd,chd->hrc", query_heads, key_heads, preferred_element_type=F32)
        / head_width**0.5
    )
    scores = jnp.where(allowed[None], scores, MASKED)
    weights = jax.nn.softmax(scores, axis=-1).astype(BF)
    mixed = jnp.einsum("hrc,chd->rhd", weights, value_heads, preferred_element_type=F32)
    return mixed.reshape(row_count, head_count * head_width).astype(BF)


def dot(left, right):
    return jnp.dot(left, right, preferred_element_type=F32)


def contract_last(left, right):
    return lax.dot_general(left, right, (((1,), (1,)), ((), ())), preferred_element_type=F32)


def contract_first(left, right):
    return lax.dot_general(left, right, (((0,), (0,)), ((), ())), preferred_element_type=F32)


def seq_swap(value, bits):
    return lax.ppermute(value, "seq", [(i, i ^ bits) for i in range(lax.axis_size("seq"))])


def mp_swap(value, bits):
    return lax.ppermute(value, "mp", [(i, i ^ bits) for i in range(lax.axis_size("mp"))])


def gather_mp(value):
    return [value] + [mp_swap(value, k) for k in range(1, lax.axis_size("mp"))]


def exchange_mp(pieces):
    return [pieces[0]] + [mp_swap(pieces[k], k) for k in range(1, len(pieces))]


def gather_seq(value):
    out = []
    for chip in range(lax.axis_size("seq") // 2):
        same = value if chip == 0 else seq_swap(value, 2 * chip)
        out += [same, seq_swap(same, 1)]
    return out


def exchange_seq(blocks):
    chips = blocks.shape[0]
    got = [blocks[0]] + [seq_swap(blocks[i], 2 * i) for i in range(1, chips)]
    mine = jnp.stack([piece[0] for piece in got])
    other = seq_swap(jnp.stack([piece[1] for piece in got]), 1)
    return jnp.stack([mine, other], axis=1)


def scatter_sum_seq(partial):
    size = lax.axis_size("seq")
    here = lax.axis_index("seq")
    rows = partial.shape[0] // size

    def block(j):
        return lax.dynamic_slice_in_dim(partial, (here ^ j) * rows, rows, 0)

    total = None
    for chip in list(range(1, size // 2)) + [0]:
        arrived = seq_swap(block(2 * chip + 1), 1)
        summed = block(2 * chip).astype(F32) + arrived.astype(F32)
        if chip:
            summed = seq_swap(summed.astype(BF), 2 * chip).astype(F32)
        total = summed if total is None else total + summed
    return total


def place_rows(blocks):
    here = lax.axis_index("seq")
    rows = blocks[0].shape[0]
    out = jnp.zeros((rows * len(blocks), blocks[0].shape[1]), blocks[0].dtype)
    for j, block in enumerate(blocks):
        out = lax.dynamic_update_slice_in_dim(out, block, (here ^ j) * rows, 0)
    return out


def call_on_blocks(body, scalars, operands, outs, scratch, flops, moved):
    whole = pl.BlockSpec(memory_space=pltpu.VMEM)
    return pl.pallas_call(
        body,
        out_shape=outs,
        in_specs=[pl.BlockSpec(memory_space=pltpu.SMEM)] + [whole] * len(operands),
        out_specs=[whole] * len(outs),
        scratch_shapes=scratch,
        compiler_params=pltpu.CompilerParams(vmem_limit_bytes=48 * 1024 * 1024),
        cost_estimate=pl.CostEstimate(flops=flops, bytes_accessed=moved, transcendentals=0),
    )(scalars, *operands)


def block_rows(total, most):
    best = total
    for step in range(16, most + 1, 16):
        if total % step == 0:
            best = step
    return best


def partial_blocks(weight_t, wide):
    size = lax.axis_size("seq")
    rows = weight_t.shape[0] // size
    depth = weight_t.shape[1]
    width = sum(piece.shape[0] for piece in wide)
    chips = size // 2
    piece_rows = wide[0].shape[0]

    def body(place_ref, low_ref, high_ref, *refs):
        wide_refs, mine_ref, other_ref = refs[:-2], refs[-2], refs[-1]
        for left_ref, out_ref in ((low_ref, mine_ref), (high_ref, other_ref)):
            left = left_ref[...]
            for n, wide_ref in enumerate(wide_refs):
                out_ref[0, :, n * piece_rows : (n + 1) * piece_rows] = contract_last(
                    left, wide_ref[...]
                ).astype(BF)

    here = lax.axis_index("seq").astype(jnp.int32)
    spec = pltpu.PrefetchScalarGridSpec(
        num_scalar_prefetch=1,
        grid=(chips,),
        in_specs=[
            pl.BlockSpec((rows, depth), lambda i, place: (place[0] ^ (2 * i), 0)),
            pl.BlockSpec((rows, depth), lambda i, place: (place[0] ^ (2 * i + 1), 0)),
        ]
        + [pl.BlockSpec((piece_rows, depth), lambda i, place: (0, 0))] * len(wide),
        out_specs=[pl.BlockSpec((1, rows, width), lambda i, place: (i, 0, 0))] * 2,
    )
    shape = jax.ShapeDtypeStruct((chips, rows, width), BF)
    return pl.pallas_call(
        body,
        grid_spec=spec,
        out_shape=[shape, shape],
        compiler_params=pltpu.CompilerParams(vmem_limit_bytes=32 * 1024 * 1024),
        cost_estimate=pl.CostEstimate(
            flops=2 * size * rows * width * depth,
            bytes_accessed=2 * size * rows * (width + depth),
            transcendentals=0,
        ),
    )(here[None], weight_t, weight_t, *wide)


def scatter_blocks(mine, other):
    arrived = seq_swap(other, 1)
    summed = mine.astype(F32) + arrived.astype(F32)
    total = summed[0]
    for chip in range(1, mine.shape[0]):
        total = total + seq_swap(summed[chip].astype(BF), 2 * chip).astype(F32)
    return total


def sort_cot(got, count, lane_index):
    lanes = len(got)
    per_lane, slots, sub = got[0].shape
    chips = lanes * per_lane // 2

    def body(table_ref, *refs):
        got_refs, out_refs = refs[:lanes], refs[lanes:]
        for i, out_ref in enumerate(out_refs):
            for t in range(2):
                place = table_ref[0] ^ (2 * i + t)
                source = (place // per_lane) ^ table_ref[1]
                value = got_refs[0][place % per_lane]
                for k in range(1, lanes):
                    value = jnp.where(source == k, got_refs[k][place % per_lane], value)
                out_ref[t, :slots, :] = value
                out_ref[t, slots:, :] = jnp.full((16, sub), table_ref[2].astype(F32)).astype(BF)

    table = jnp.stack([lax.axis_index("seq"), lane_index, count]).astype(jnp.int32)
    out = jax.ShapeDtypeStruct((2, slots + 16, sub), BF)
    return call_on_blocks(body, table, got, [out] * chips, [], 0, 8 * chips * slots * sub)


def exchange_pieces(blocks):
    mine = [blocks[0]] + [seq_swap(blocks[i], 2 * i) for i in range(1, len(blocks))]
    return mine, [seq_swap(piece, 1) for piece in mine]


def pack_cot(mine, other, total_rows):
    chips = len(mine)
    size = 2 * chips
    sub = mine[0].shape[2]
    slots = mine[0].shape[1] - 16

    def body(place_ref, *refs):
        mine_refs, other_refs = refs[:chips], refs[chips:size]
        packed_ref, table_ref = refs[size:]
        blocks = [(refs_of[j // 2], j % 2) for j, refs_of in enumerate([mine_refs, other_refs] * chips)]
        counts = [ref[t, slots : slots + 1, 0:1].astype(F32) for ref, t in blocks]
        row = lax.broadcasted_iota(jnp.int32, (total_rows, slots), 0)
        slot = lax.broadcasted_iota(jnp.int32, (total_rows, slots), 1)
        gap = (row - slot).astype(F32)
        slot = slot.astype(F32)
        total = jnp.zeros((total_rows, sub), F32)
        for j, (ref, t) in enumerate(blocks):
            offset = jnp.zeros((1, 1), F32)
            for n in range(size):
                before = (place_ref[0] ^ n) < (place_ref[0] ^ j)
                offset = offset + jnp.where(before, counts[n], 0.0)
            spread = jnp.where((gap == offset) & (slot < counts[j]), 1.0, 0.0).astype(BF)
            total = total + dot(spread, ref[t, :slots, :])
            table_ref[j : j + 1, :] = jnp.broadcast_to(offset, (1, 128)).astype(jnp.int32)
            table_ref[size + j : size + j + 1, :] = jnp.broadcast_to(counts[j], (1, 128)).astype(
                jnp.int32
            )
        packed_ref[...] = total.astype(BF)

    place = lax.axis_index("seq").astype(jnp.int32)[None]
    packed, table = call_on_blocks(
        body,
        place,
        mine + other,
        [
            jax.ShapeDtypeStruct((total_rows, sub), BF),
            jax.ShapeDtypeStruct((2 * size, 128), jnp.int32),
        ],
        [],
        2 * size * slots * total_rows * sub,
        8 * size * slots * sub,
    )
    return packed, table[:, 0]


def hidden_kernel(lifted, mixed, enc_pieces, table, lane_index, total_rows, sub):
    rows = lifted.shape[0]
    slots = mixed[0].shape[0]
    size = len(mixed)
    piece = enc_pieces[0].shape[0]

    def body(table_ref, lifted_ref, *refs):
        mixed_refs, enc_refs = refs[:size], refs[size : size + len(enc_pieces)]
        pre_ref, hidden_ref, rows_ref, stack_ref, spread_ref = refs[size + len(enc_pieces) :]
        lane = pl.multiple_of(table_ref[2 * size] * sub, sub)
        left = lifted_ref[...]
        slot = lax.broadcasted_iota(jnp.int32, (slots, total_rows), 0)
        gap = lax.broadcasted_iota(jnp.int32, (slots, total_rows), 1) - slot
        for j in range(size):
            spread_ref[j * slots : (j + 1) * slots, :] = jnp.where(
                (gap == table_ref[j]) & (slot < table_ref[size + j]), 1.0, 0.0
            ).astype(BF)
        for i in range(size // 2):
            slot_pre = jnp.concatenate(
                [contract_last(left, mixed_refs[2 * i + t][...]) for t in range(2)], axis=1
            )
            high = slot_pre.astype(BF)
            columns = slice(2 * i * slots, 2 * (i + 1) * slots)
            stack_ref[:rows, columns] = jax.nn.gelu(slot_pre).astype(BF)
            stack_ref[rows : 2 * rows, columns] = high
            stack_ref[2 * rows :, columns] = (slot_pre - high.astype(F32)).astype(BF)
        hidden_ref[...] = dot(stack_ref[:rows, :], spread_ref[...]).astype(BF)
        pre_ref[...] = dot(stack_ref[rows : 2 * rows, :], spread_ref[...]) + dot(
            stack_ref[2 * rows :, :], spread_ref[...]
        )
        for j, mixed_ref in enumerate(mixed_refs):
            patch = jnp.zeros((slots, sub), F32)
            for n, enc_ref in enumerate(enc_refs):
                patch = patch + dot(
                    mixed_ref[:, n * piece : (n + 1) * piece], enc_ref[:, pl.ds(lane, sub)]
                )
            rows_ref[j * slots : (j + 1) * slots, :] = patch.astype(BF)

    table = jnp.concatenate([table, lane_index.astype(jnp.int32)[None]])
    width = lifted.shape[1]
    return call_on_blocks(
        body,
        table,
        [lifted] + mixed + enc_pieces,
        [
            jax.ShapeDtypeStruct((rows, total_rows), F32),
            jax.ShapeDtypeStruct((rows, total_rows), BF),
            jax.ShapeDtypeStruct((size * slots, sub), BF),
        ],
        [pltpu.VMEM((3 * rows, size * slots), BF), pltpu.VMEM((size * slots, total_rows), BF)],
        2 * size * slots * (rows * (width + 3 * total_rows) + width * sub),
        2 * (size * slots * width + 3 * rows * total_rows),
    )


def unpack_home(parts, rows_own, table, slots):
    count = len(parts)
    size = table.shape[0] // 2
    total_rows, sub = parts[0].shape
    extra = [] if rows_own is None else [rows_own]

    def body(table_ref, *refs):
        total = refs[0][...].astype(F32)
        for ref in refs[1:count]:
            total = total + ref[...].astype(F32)
        total = total.astype(BF)
        slot = lax.broadcasted_iota(jnp.int32, (slots, total_rows), 0)
        gap = lax.broadcasted_iota(jnp.int32, (slots, total_rows), 1) - slot
        outs = refs[count + len(extra) :]
        for j in range(size):
            live = slot < table_ref[size + j]
            spread = jnp.where((gap == table_ref[j]) & live, 1.0, 0.0).astype(BF)
            home = dot(spread, total)
            if extra:
                own = refs[count][j * slots : (j + 1) * slots, :].astype(F32)
                home = home + jnp.where(live[:, :sub], own, 0.0)
            outs[j // 2][j % 2] = home.astype(BF)

    out = jax.ShapeDtypeStruct((2, slots, sub), BF)
    return call_on_blocks(
        body,
        table,
        parts + extra,
        [out] * (size // 2),
        [],
        2 * size * slots * total_rows * sub,
        2 * (count * total_rows + 2 * size * slots) * sub,
    )


def keys_values(mine, other, weights, lanes):
    chips = len(mine)
    _, slots, sub = mine[0].shape
    width = weights[0].shape[2]

    def body(place_ref, *refs):
        mine_refs, other_refs, weight_refs = refs[:chips], refs[chips : 2 * chips], refs[2 * chips : 4 * chips]
        out_refs = refs[4 * chips :]
        for k, out_ref in enumerate(out_refs):
            total = jnp.zeros((slots, width), F32)
            for j, weight_ref in enumerate(weight_refs):
                ref = (mine_refs, other_refs)[j % 2][j // 2]
                total = total + dot(ref[j % 2], weight_ref[k])
            out_ref[...] = total.astype(BF)

    return call_on_blocks(
        body,
        jnp.zeros((1,), jnp.int32),
        mine + other + weights,
        [jax.ShapeDtypeStruct((slots, width), BF)] * lanes,
        [],
        4 * chips * slots * sub * lanes * width,
        4 * chips * sub * lanes * width,
    )


def sort_grad(mine, other, lanes, lane_index):
    chips = len(mine)
    _, slots, sub = mine[0].shape
    per_lane = 2 * chips // lanes

    def body(place_ref, *refs):
        mine_refs, other_refs = refs[:chips], refs[chips : 2 * chips]
        for k, out_ref in enumerate(refs[2 * chips :]):
            for p in range(per_lane):
                place = ((place_ref[1] ^ k) * per_lane + p) ^ place_ref[0]
                value = mine_refs[0][0]
                for j in range(1, 2 * chips):
                    block = (mine_refs, other_refs)[j % 2][j // 2][j % 2]
                    value = jnp.where(place == j, block, value)
                out_ref[p] = value

    place = jnp.stack([lax.axis_index("seq"), lane_index]).astype(jnp.int32)
    out = jax.ShapeDtypeStruct((per_lane, slots, sub), BF)
    return call_on_blocks(body, place, mine + other, [out] * lanes, [], 0, 8 * chips * slots * sub)


def finish_grad(cot, got, count, lane_index):
    lanes = len(got)
    per_lane, slots, sub = got[0].shape

    def body(place_ref, cot_ref, *refs):
        live = lax.broadcasted_iota(jnp.int32, (slots, sub), 0) < place_ref[1]
        for k in range(lanes):
            for p in range(per_lane):
                columns = pl.ds(pl.multiple_of((p * lanes + (place_ref[0] ^ k)) * sub, sub), sub)
                total = cot_ref[:, columns].astype(F32) + refs[k][p].astype(F32)
                refs[lanes][:, columns] = jnp.where(live, total, 0.0).astype(BF)

    place = jnp.stack([lane_index, count]).astype(jnp.int32)
    return call_on_blocks(
        body, place, [cot] + got, [jax.ShapeDtypeStruct(cot.shape, BF)], [], 0, 6 * cot.size
    )[0]


def mix_pieces(pieces, weight_t, lane_index):
    size = len(pieces)
    lanes = lax.axis_size("mp")
    rows, total_rows = pieces[0].shape
    width = weight_t.shape[1]
    sub = width // lanes
    step = 256 if total_rows % 256 == 0 else total_rows

    def body(place_ref, weight_ref, *refs):
        piece_refs, out_refs, acc_ref = refs[:size], refs[size:-1], refs[-1]
        total = None
        for j, piece_ref in enumerate(piece_refs):
            start = pl.multiple_of((place_ref[0] ^ j) * rows, 16)
            part = contract_first(piece_ref[...], weight_ref[pl.ds(start, rows), :])
            total = part if total is None else total + part
        acc_ref[...] = total
        for k, out_ref in enumerate(out_refs):
            start = pl.multiple_of((place_ref[1] ^ k) * sub, sub)
            out_ref[...] = acc_ref[:, pl.ds(start, sub)].astype(BF)

    place = jnp.stack([lax.axis_index("seq"), lane_index]).astype(jnp.int32)
    spec = pltpu.PrefetchScalarGridSpec(
        num_scalar_prefetch=1,
        grid=(total_rows // step,),
        in_specs=[pl.BlockSpec(weight_t.shape, lambda r, place: (0, 0))]
        + [pl.BlockSpec((rows, step), lambda r, place: (0, r))] * size,
        out_specs=[pl.BlockSpec((step, sub), lambda r, place: (r, 0))] * lanes,
        scratch_shapes=[pltpu.VMEM((step, width), F32)],
    )
    return pl.pallas_call(
        body,
        grid_spec=spec,
        out_shape=[jax.ShapeDtypeStruct((total_rows, sub), BF)] * lanes,
        compiler_params=pltpu.CompilerParams(vmem_limit_bytes=32 * 1024 * 1024),
        cost_estimate=pl.CostEstimate(
            flops=2 * size * rows * total_rows * width,
            bytes_accessed=2 * (size * rows * (total_rows + width) + total_rows * width),
            transcendentals=0,
        ),
    )(place, weight_t, *pieces)


def outer_pieces(cot_lanes, pieces, lane_index, scale):
    size = len(pieces)
    lanes = len(cot_lanes)
    rows, total_rows = pieces[0].shape
    sub = cot_lanes[0].shape[1]
    full = size * rows
    step = block_rows(full, 256) if full % 256 else 256

    def body(place_ref, *refs):
        cot_refs, piece_refs = refs[:lanes], refs[lanes : lanes + size]
        out_ref, acc_ref = refs[lanes + size :]
        for j, piece_ref in enumerate(piece_refs):
            start = pl.multiple_of((place_ref[0] ^ j) * rows, 16)
            left = piece_ref[...]
            for k, cot_ref in enumerate(cot_refs):
                acc_ref[pl.ds(start, rows), k * sub : (k + 1) * sub] = dot(left, cot_ref[...]) * scale
        for k in range(lanes):
            top = pl.multiple_of((place_ref[1] ^ k) * sub, sub)
            for n in range(full // step):
                block = acc_ref[n * step : (n + 1) * step, k * sub : (k + 1) * sub]
                out_ref[pl.ds(top, sub), n * step : (n + 1) * step] = block.T.astype(BF)

    place = jnp.stack([lax.axis_index("seq"), lane_index]).astype(jnp.int32)
    return call_on_blocks(
        body,
        place,
        cot_lanes + pieces,
        [jax.ShapeDtypeStruct((lanes * sub, full), BF)],
        [pltpu.VMEM((full, lanes * sub), F32)],
        2 * full * total_rows * lanes * sub,
        2 * (full * total_rows + total_rows * lanes * sub + full * lanes * sub),
    )[0]


def per_device(
    byte_states,
    patch_starts,
    patch_counts,
    patch_owner,
    enc_query,
    enc_key,
    enc_value,
    enc_out,
    up_proj,
    down_proj,
    dec_query,
    dec_key,
    dec_value,
    dec_out,
    latent_cotangent,
):
    groups = lax.axis_size("seq")
    chips = groups // 2
    lanes = lax.axis_size("mp")
    here = lax.axis_index("seq")
    lane_index = lax.axis_index("mp")
    byte_count = byte_states.shape[0]
    slots = patch_starts.shape[1]
    total_rows = groups * CAP
    slice_width = up_proj.shape[0]
    sub = slice_width // lanes
    per_lane = groups // lanes
    patch_start = patch_starts[0]
    patch_total = patch_counts[0, 0]
    hidden_rows = up_proj.shape[1] // groups
    tiled = hidden_rows % 16 == 0 and sub % 128 == 0 and slots % 64 == 0 and groups <= 8
    scope = jax.named_scope
    scale = 1.0 / math.sqrt(total_rows)
    relative = jnp.arange(groups, dtype=jnp.int32) ^ here
    slot_ids = jnp.arange(slots, dtype=jnp.int32)
    positions = jnp.arange(byte_count, dtype=jnp.int32)

    with scope("encz"):
        enc_own = lax.dynamic_slice_in_dim(enc_out, here * slice_width, slice_width, 1)
        enc_pieces = gather_mp(enc_own)

    def cot_piece(k):
        return jnp.stack(
            [
                lax.dynamic_slice_in_dim(
                    latent_cotangent, (p * lanes + (lane_index ^ k)) * sub, sub, 1
                )
                for p in range(per_lane)
            ]
        )

    with scope("cotz"):
        cot_got = exchange_mp([cot_piece(k) for k in range(lanes)])

    if tiled:
        with scope("flip_up"):
            up_t = up_proj.T
        with scope("eukern"):
            lifted_parts = partial_blocks(up_t, enc_pieces)
        with scope("eux"):
            lifted = scatter_blocks(*lifted_parts).astype(BF)
        with scope("cotsort"):
            cot_sent = sort_cot(cot_got, patch_total, lane_index)
        with scope("cotx"):
            cot_mine, cot_other = exchange_pieces(cot_sent)
        with scope("cotpack"):
            cot_packed, table = pack_cot(cot_mine, cot_other, total_rows)
    else:
        enc_slice = jnp.concatenate(enc_pieces, axis=0)
        lifted_part = lax.dot_general(
            up_proj, enc_slice, (((0,), (1,)), ((), ())), preferred_element_type=F32
        ).astype(BF)
        lifted = scatter_sum_seq(lifted_part).astype(BF)
        cot_sent = jnp.full((groups, slots + 16, sub), patch_total.astype(F32).astype(BF))
        for k in range(lanes):
            for p in range(per_lane):
                place = ((lane_index ^ k) * per_lane + p) ^ here
                cot_sent = lax.dynamic_update_slice(cot_sent, cot_got[k][p][None], (place, 0, 0))
        cot_here = exchange_seq(cot_sent.reshape(chips, 2, slots + 16, sub)).reshape(
            groups, slots + 16, sub
        )
        counts = cot_here[:, slots, 0].astype(F32).astype(jnp.int32)
        before = relative[None, :] < relative[:, None]
        offsets = jnp.sum(jnp.where(before, counts[None, :], 0), axis=1)
        places = jnp.where(
            slot_ids[None, :] < counts[:, None], offsets[:, None] + slot_ids[None, :], -1
        ).reshape(groups * slots)
        row_ids = jnp.arange(total_rows, dtype=jnp.int32)
        selector = (row_ids[:, None] == places[None, :]).astype(BF)
        cot_packed = dot(selector, cot_here[:, :slots].reshape(groups * slots, sub)).astype(BF)

    with scope("cotag"):
        cot_all = gather_mp(cot_packed)
        cot_slice = jnp.zeros((total_rows, slice_width), BF)
        for k in range(lanes):
            cot_slice = lax.dynamic_update_slice_in_dim(
                cot_slice, cot_all[k], (lane_index ^ k) * sub, 1
            )

    with scope("encode"):
        patch_end = jnp.concatenate([patch_start[1:], jnp.full((1,), byte_count, jnp.int32)])
        member = (positions[None, :] >= patch_start[:, None]) & (
            positions[None, :] < patch_end[:, None]
        )
        lengths = jnp.sum(member.astype(F32), axis=1)
        pooled = dot(member.astype(BF), byte_states)
        pooled = (pooled / jnp.maximum(lengths, 1.0)[:, None]).astype(BF)
        queries = dot(pooled, enc_query).astype(BF)
        keys_in = dot(byte_states, enc_key).astype(BF)
        values_in = dot(byte_states, enc_value).astype(BF)
        mixed = attend(queries, keys_in, values_in, member, enc_query.shape[1] // HD)
    with scope("mixz"):
        mixed = jnp.concatenate(gather_mp(mixed), axis=1)
    with scope("mixx"):
        mixed_pieces = gather_seq(mixed)

    def sum_parts(got):
        total = got[0].astype(F32)
        for piece in got[1:]:
            total = total + piece.astype(F32)
        return total

    with scope("decwz"):
        rows_of = lambda weight, k: lax.dynamic_slice_in_dim(
            weight, here * slice_width + (lane_index ^ k) * sub, sub, 0
        )
        head_pieces = exchange_mp(
            [
                jnp.concatenate([rows_of(dec_key, k), rows_of(dec_value, k)], axis=1)
                for k in range(lanes)
            ]
        )
        head_weights = jnp.stack(head_pieces)
    with scope("decwx"):
        head_weights = gather_seq(head_weights)

    if tiled:
        with scope("hidkern"):
            hidden_pre, hidden, rows_own = hidden_kernel(
                lifted, mixed_pieces, enc_pieces, table, lane_index, total_rows, sub
            )
        with scope("hidx"):
            hidden_pieces = gather_seq(hidden)
        with scope("flip_down"):
            down_t = down_proj.T
        with scope("fwdkern"):
            forward_blocks = mix_pieces(hidden_pieces, down_t, lane_index)
        with scope("outz"):
            forward_got = exchange_mp(forward_blocks)
        with scope("dgkern"):
            down_grad = outer_pieces(cot_all, hidden_pieces, lane_index, scale)
        with scope("backkern"):
            backward_parts = partial_blocks(down_t, [cot_slice])
        with scope("backx"):
            backward = scatter_blocks(*backward_parts)
        with scope("innact"):
            inner = gelu_back(hidden_pre, backward).astype(BF)
        with scope("innx"):
            inner_pieces = gather_seq(inner)
        with scope("gkern"):
            backward_blocks = mix_pieces(inner_pieces, up_t, lane_index)
        with scope("gradz"):
            backward_got = exchange_mp(backward_blocks)
        with scope("unpack"):
            latent_sent = unpack_home(forward_got, rows_own, table, slots)
        with scope("homex"):
            latent_mine, latent_other = exchange_pieces(latent_sent)
        with scope("kvkern"):
            terms = keys_values(latent_mine, latent_other, head_weights, lanes)
    else:
        mixed_all = jnp.concatenate(mixed_pieces, axis=0)
        slot_pre = contract_last(lifted, mixed_all)
        slot_hidden = jax.nn.gelu(slot_pre).astype(BF)
        hidden = contract_last(slot_hidden, selector).astype(BF)
        hidden_all = place_rows(gather_seq(hidden))
        forward_part = lax.dot_general(
            hidden_all, down_proj, (((0,), (1,)), ((), ())), preferred_element_type=F32
        ).astype(BF)
        pre_high = slot_pre.astype(BF)
        pre_low = (slot_pre - pre_high.astype(F32)).astype(BF)
        hidden_pre = contract_last(pre_high, selector) + contract_last(pre_low, selector)
        backward_partial = lax.dot_general(
            down_proj, cot_slice, (((0,), (1,)), ((), ())), preferred_element_type=F32
        ).astype(BF)
        backward = scatter_sum_seq(backward_partial)
        inner = gelu_back(hidden_pre, backward).astype(BF)
        inner_all = place_rows(gather_seq(inner))
        backward_part = lax.dot_general(
            inner_all, up_proj, (((0,), (1,)), ((), ())), preferred_element_type=F32
        ).astype(BF)
        down_grad = lax.dot_general(
            cot_slice, hidden_all, (((0,), (1,)), ((), ())), preferred_element_type=F32
        )
        down_grad = (down_grad * scale).astype(BF)

        def sum_lanes(part):
            blocks = [
                lax.dynamic_slice_in_dim(part, (lane_index ^ k) * sub, sub, 1) for k in range(lanes)
            ]
            return sum_parts(exchange_mp(blocks)).astype(BF)

        def send_home(home):
            return exchange_seq(home.astype(BF).reshape(chips, 2, slots, sub)).reshape(
                groups, slots, sub
            )

        enc_sub = lax.dynamic_slice_in_dim(enc_slice, lane_index * sub, sub, 1)
        rows_own = jnp.where((places >= 0)[:, None], dot(mixed_all, enc_sub), 0.0)
        latent_here = send_home(contract_first(selector, sum_lanes(forward_part)) + rows_own)
        terms = []
        for k in range(lanes):
            term = sum(dot(latent_here[j], head_weights[j][k]) for j in range(groups))
            terms.append(term.astype(BF))

    with scope("kvz"):
        both = sum_parts(exchange_mp(terms)).astype(BF)
    with scope("decq"):
        dec_queries = dot(byte_states, dec_query).astype(BF)
    with scope("decode"):
        dec_keys = both[:, : dec_key.shape[1]]
        dec_values = both[:, dec_key.shape[1] :]
        home_patch = (
            jnp.sum((patch_start[None, :] <= positions[:, None]).astype(jnp.int32), axis=1) - 1
        )
        allowed = slot_ids[None, :] <= home_patch[:, None]
        byte_mixed = attend(dec_queries, dec_keys, dec_values, allowed, dec_query.shape[1] // HD)
        decoded_part = dot(byte_mixed, dec_out).astype(BF)
    with scope("decz"):
        width_here = decoded_part.shape[1] // lanes
        got = exchange_mp(
            [
                lax.dynamic_slice_in_dim(decoded_part, (lane_index ^ k) * width_here, width_here, 1)
                for k in range(lanes)
            ]
        )
        own_cols = lax.dynamic_slice_in_dim(byte_states, lane_index * width_here, width_here, 1)
        decoded = (own_cols.astype(F32) + sum_parts(got)).astype(BF)

    if tiled:
        with scope("gunpack"):
            grad_sent = unpack_home(backward_got, None, table, slots)
        with scope("ghomex"):
            grad_mine, grad_other = exchange_pieces(grad_sent)
        with scope("gsort"):
            grad_out = sort_grad(grad_mine, grad_other, lanes, lane_index)
        with scope("gradag"):
            grad_got = exchange_mp(grad_out)
        with scope("gfinish"):
            patch_grad = finish_grad(latent_cotangent, grad_got, patch_total, lane_index)
        return (decoded, patch_grad, down_grad)

    grad_here = send_home(contract_first(selector, sum_lanes(backward_part)))

    def grad_piece(k):
        return jnp.stack(
            [
                lax.dynamic_index_in_dim(
                    grad_here, ((lane_index ^ k) * per_lane + p) ^ here, 0, keepdims=False
                )
                for p in range(per_lane)
            ]
        )

    grad_got = exchange_mp([grad_piece(k) for k in range(lanes)])
    grad_cols = jnp.zeros((slots, lanes * per_lane * sub), BF)
    for k in range(lanes):
        for p in range(per_lane):
            grad_cols = lax.dynamic_update_slice_in_dim(
                grad_cols, grad_got[k][p], (p * lanes + (lane_index ^ k)) * sub, 1
            )
    live = patch_owner[0] >= 0
    patch_grad = latent_cotangent.astype(F32) + grad_cols.astype(F32)
    patch_grad = jnp.where(live[:, None], patch_grad, 0.0).astype(BF)
    return (decoded, patch_grad, down_grad)


def solution(mesh):
    return jax.shard_map(
        per_device,
        mesh=mesh,
        in_specs=(
            P("seq", None),
            P("seq", None),
            P("seq", None),
            P("seq", None),
            P(None, "mp"),
            P(None, "mp"),
            P(None, "mp"),
            P("mp", None),
            P("seq", "mp"),
            P("seq", "mp"),
            P(None, "mp"),
            P(None, "mp"),
            P(None, "mp"),
            P("mp", None),
            P("seq", "mp"),
        ),
        out_specs=(P("seq", "mp"), P("seq", "mp"), P("seq", "mp")),
        check_vma=False,
    )
```

```python
import math

import jax
import jax.numpy as jnp
from jax import lax
from jax.experimental import pallas as pl
from jax.experimental.pallas import tpu as pltpu
from jax.sharding import PartitionSpec as P

HD = 64
CAP = 128
MASKED = -1e30


BF = jnp.bfloat16
F32 = jnp.float32


def gelu_back(hidden_pre, incoming):
    return jax.vjp(jax.nn.gelu, hidden_pre)[1](incoming)[0]


def attend(queries, keys_in, values_in, allowed, head_count):
    row_count = queries.shape[0]
    col_count = keys_in.shape[0]
    head_width = queries.shape[1] // head_count
    query_heads = queries.reshape(row_count, head_count, head_width)
    key_heads = keys_in.reshape(col_count, head_count, head_width)
    value_heads = values_in.reshape(col_count, head_count, head_width)
    scores = (
        jnp.einsum("rhd,chd->hrc", query_heads, key_heads, preferred_element_type=F32)
        / head_width**0.5
    )
    scores = jnp.where(allowed[None], scores, MASKED)
    weights = jax.nn.softmax(scores, axis=-1).astype(BF)
    mixed = jnp.einsum("hrc,chd->rhd", weights, value_heads, preferred_element_type=F32)
    return mixed.reshape(row_count, head_count * head_width).astype(BF)


def dot(left, right):
    return jnp.dot(left, right, preferred_element_type=F32)


def contract_last(left, right):
    return lax.dot_general(left, right, (((1,), (1,)), ((), ())), preferred_element_type=F32)


def contract_first(left, right):
    return lax.dot_general(left, right, (((0,), (0,)), ((), ())), preferred_element_type=F32)


def seq_swap(value, bits):
    return lax.ppermute(value, "seq", [(i, i ^ bits) for i in range(lax.axis_size("seq"))])


def mp_swap(value, bits):
    return lax.ppermute(value, "mp", [(i, i ^ bits) for i in range(lax.axis_size("mp"))])


def gather_mp(value):
    return [value] + [mp_swap(value, k) for k in range(1, lax.axis_size("mp"))]


def exchange_mp(pieces):
    return [pieces[0]] + [mp_swap(pieces[k], k) for k in range(1, len(pieces))]


def gather_seq(value):
    out = []
    for chip in range(lax.axis_size("seq") // 2):
        same = value if chip == 0 else seq_swap(value, 2 * chip)
        out += [same, seq_swap(same, 1)]
    return out


def exchange_seq(blocks):
    chips = blocks.shape[0]
    got = [blocks[0]] + [seq_swap(blocks[i], 2 * i) for i in range(1, chips)]
    mine = jnp.stack([piece[0] for piece in got])
    other = seq_swap(jnp.stack([piece[1] for piece in got]), 1)
    return jnp.stack([mine, other], axis=1)


def scatter_sum_seq(partial):
    size = lax.axis_size("seq")
    here = lax.axis_index("seq")
    rows = partial.shape[0] // size

    def block(j):
        return lax.dynamic_slice_in_dim(partial, (here ^ j) * rows, rows, 0)

    total = None
    for chip in list(range(1, size // 2)) + [0]:
        arrived = seq_swap(block(2 * chip + 1), 1)
        summed = block(2 * chip).astype(F32) + arrived.astype(F32)
        if chip:
            summed = seq_swap(summed.astype(BF), 2 * chip).astype(F32)
        total = summed if total is None else total + summed
    return total


def place_rows(blocks):
    here = lax.axis_index("seq")
    rows = blocks[0].shape[0]
    out = jnp.zeros((rows * len(blocks), blocks[0].shape[1]), blocks[0].dtype)
    for j, block in enumerate(blocks):
        out = lax.dynamic_update_slice_in_dim(out, block, (here ^ j) * rows, 0)
    return out


def call_on_blocks(body, scalars, operands, outs, scratch, flops, moved):
    whole = pl.BlockSpec(memory_space=pltpu.VMEM)
    return pl.pallas_call(
        body,
        out_shape=outs,
        in_specs=[pl.BlockSpec(memory_space=pltpu.SMEM)] + [whole] * len(operands),
        out_specs=[whole] * len(outs),
        scratch_shapes=scratch,
        compiler_params=pltpu.CompilerParams(vmem_limit_bytes=48 * 1024 * 1024),
        cost_estimate=pl.CostEstimate(flops=flops, bytes_accessed=moved, transcendentals=0),
    )(scalars, *operands)


def block_rows(total, most):
    best = total
    for step in range(16, most + 1, 16):
        if total % step == 0:
            best = step
    return best


def partial_blocks(weight_t, wide, lane_index=None):
    size = lax.axis_size("seq")
    rows = weight_t.shape[0] // size
    depth = weight_t.shape[1]
    chips = size // 2
    piece_rows, sub = wide[0].shape
    by_columns = lane_index is not None
    width = piece_rows if by_columns else piece_rows * len(wide)

    def body(place_ref, low_ref, high_ref, *refs):
        count = len(wide)
        wide_refs, mine_ref, other_ref = refs[:count], refs[count], refs[count + 1]
        if by_columns:
            right_ref = refs[count + 2]

            @pl.when(pl.program_id(0) == 0)
            def _():
                for k, wide_ref in enumerate(wide_refs):
                    start = pl.multiple_of((place_ref[1] ^ k) * sub, sub)
                    right_ref[:, pl.ds(start, sub)] = wide_ref[...]

            wide_refs = [right_ref]
        for left_ref, out_ref in ((low_ref, mine_ref), (high_ref, other_ref)):
            left = left_ref[...]
            for n, wide_ref in enumerate(wide_refs):
                out_ref[0, :, n * piece_rows : (n + 1) * piece_rows] = contract_last(
                    left, wide_ref[...]
                ).astype(BF)

    lane = lane_index if by_columns else lax.axis_index("mp")
    place = jnp.stack([lax.axis_index("seq"), lane]).astype(jnp.int32)
    spec = pltpu.PrefetchScalarGridSpec(
        num_scalar_prefetch=1,
        grid=(chips,),
        in_specs=[
            pl.BlockSpec((rows, depth), lambda i, place: (place[0] ^ (2 * i), 0)),
            pl.BlockSpec((rows, depth), lambda i, place: (place[0] ^ (2 * i + 1), 0)),
        ]
        + [pl.BlockSpec((piece_rows, sub), lambda i, place: (0, 0))] * len(wide),
        out_specs=[pl.BlockSpec((1, rows, width), lambda i, place: (i, 0, 0))] * 2,
        scratch_shapes=[pltpu.VMEM((width, depth), BF)] if by_columns else [],
    )
    shape = jax.ShapeDtypeStruct((chips, rows, width), BF)
    return pl.pallas_call(
        body,
        grid_spec=spec,
        out_shape=[shape, shape],
        compiler_params=pltpu.CompilerParams(vmem_limit_bytes=32 * 1024 * 1024),
        cost_estimate=pl.CostEstimate(
            flops=2 * size * rows * width * depth,
            bytes_accessed=2 * size * rows * (width + depth),
            transcendentals=0,
        ),
    )(place, weight_t, weight_t, *wide)


def add_halves(mine, other):
    chips, rows, width = mine.shape
    step = block_rows(rows, 64)

    def body(mine_ref, other_ref, *out_refs):
        for i, out_ref in enumerate(out_refs):
            total = mine_ref[i].astype(F32) + other_ref[i].astype(F32)
            out_ref[...] = total.astype(out_ref.dtype)

    whole = pl.BlockSpec((chips, step, width), lambda r: (0, r, 0))
    return pl.pallas_call(
        body,
        grid=(rows // step,),
        in_specs=[whole, whole],
        out_specs=[pl.BlockSpec((step, width), lambda r: (r, 0))] * chips,
        out_shape=[
            jax.ShapeDtypeStruct((rows, width), BF if i else F32) for i in range(chips)
        ],
        cost_estimate=pl.CostEstimate(
            flops=mine.size, bytes_accessed=8 * mine.size, transcendentals=0
        ),
    )(mine, other)


def scatter_blocks(mine, other):
    arrived = seq_swap(other, 1)
    summed = add_halves(mine, arrived)
    got = [seq_swap(summed[i], 2 * i) for i in range(1, len(summed))]
    total = summed[0]
    for piece in got:
        total = total + piece.astype(F32)
    return total


def sort_cot(got, count, lane_index):
    lanes = len(got)
    per_lane, slots, sub = got[0].shape
    chips = lanes * per_lane // 2

    def body(table_ref, *refs):
        got_refs, out_refs = refs[:lanes], refs[lanes:]
        for i, out_ref in enumerate(out_refs):
            for t in range(2):
                place = table_ref[0] ^ (2 * i + t)
                source = (place // per_lane) ^ table_ref[1]
                value = got_refs[0][place % per_lane]
                for k in range(1, lanes):
                    value = jnp.where(source == k, got_refs[k][place % per_lane], value)
                out_ref[t, :slots, :] = value
                out_ref[t, slots:, :] = jnp.full((16, sub), table_ref[2].astype(F32)).astype(BF)

    table = jnp.stack([lax.axis_index("seq"), lane_index, count]).astype(jnp.int32)
    out = jax.ShapeDtypeStruct((2, slots + 16, sub), BF)
    return call_on_blocks(body, table, got, [out] * chips, [], 0, 8 * chips * slots * sub)


def exchange_pieces(blocks):
    mine = [blocks[0]] + [seq_swap(blocks[i], 2 * i) for i in range(1, len(blocks))]
    return mine, [seq_swap(piece, 1) for piece in mine]


def pack_cot(mine, other, total_rows):
    chips = len(mine)
    size = 2 * chips
    sub = mine[0].shape[2]
    slots = mine[0].shape[1] - 16

    def body(place_ref, *refs):
        mine_refs, other_refs = refs[:chips], refs[chips:size]
        packed_ref, table_ref = refs[size:]
        blocks = [(refs_of[j // 2], j % 2) for j, refs_of in enumerate([mine_refs, other_refs] * chips)]
        counts = [ref[t, slots : slots + 1, 0:1].astype(F32) for ref, t in blocks]
        row = lax.broadcasted_iota(jnp.int32, (total_rows, slots), 0)
        slot = lax.broadcasted_iota(jnp.int32, (total_rows, slots), 1)
        gap = (row - slot).astype(F32)
        slot = slot.astype(F32)
        total = jnp.zeros((total_rows, sub), F32)
        for j, (ref, t) in enumerate(blocks):
            offset = jnp.zeros((1, 1), F32)
            for n in range(size):
                before = (place_ref[0] ^ n) < (place_ref[0] ^ j)
                offset = offset + jnp.where(before, counts[n], 0.0)
            spread = jnp.where((gap == offset) & (slot < counts[j]), 1.0, 0.0).astype(BF)
            total = total + dot(spread, ref[t, :slots, :])
            table_ref[j : j + 1, :] = jnp.broadcast_to(offset, (1, 128)).astype(jnp.int32)
            table_ref[size + j : size + j + 1, :] = jnp.broadcast_to(counts[j], (1, 128)).astype(
                jnp.int32
            )
        packed_ref[...] = total.astype(BF)

    place = lax.axis_index("seq").astype(jnp.int32)[None]
    packed, table = call_on_blocks(
        body,
        place,
        mine + other,
        [
            jax.ShapeDtypeStruct((total_rows, sub), BF),
            jax.ShapeDtypeStruct((2 * size, 128), jnp.int32),
        ],
        [],
        2 * size * slots * total_rows * sub,
        8 * size * slots * sub,
    )
    return packed, table[:, 0]


def hidden_kernel(lifted, mixed, enc_pieces, table, lane_index, total_rows, sub):
    rows = lifted.shape[0]
    slots = mixed[0].shape[0]
    size = len(mixed)
    piece = enc_pieces[0].shape[0]

    def body(table_ref, lifted_ref, *refs):
        mixed_refs, enc_refs = refs[:size], refs[size : size + len(enc_pieces)]
        pre_ref, hidden_ref, rows_ref, stack_ref, spread_ref = refs[size + len(enc_pieces) :]
        lane = pl.multiple_of(table_ref[2 * size] * sub, sub)
        left = lifted_ref[...]
        slot = lax.broadcasted_iota(jnp.int32, (slots, total_rows), 0)
        gap = lax.broadcasted_iota(jnp.int32, (slots, total_rows), 1) - slot
        for j in range(size):
            spread_ref[j * slots : (j + 1) * slots, :] = jnp.where(
                (gap == table_ref[j]) & (slot < table_ref[size + j]), 1.0, 0.0
            ).astype(BF)
        for i in range(size // 2):
            slot_pre = jnp.concatenate(
                [contract_last(left, mixed_refs[2 * i + t][...]) for t in range(2)], axis=1
            )
            high = slot_pre.astype(BF)
            columns = slice(2 * i * slots, 2 * (i + 1) * slots)
            stack_ref[:rows, columns] = jax.nn.gelu(slot_pre).astype(BF)
            stack_ref[rows : 2 * rows, columns] = high
            stack_ref[2 * rows :, columns] = (slot_pre - high.astype(F32)).astype(BF)
        hidden_ref[...] = dot(stack_ref[:rows, :], spread_ref[...]).astype(BF)
        pre_ref[...] = dot(stack_ref[rows : 2 * rows, :], spread_ref[...]) + dot(
            stack_ref[2 * rows :, :], spread_ref[...]
        )
        for j, mixed_ref in enumerate(mixed_refs):
            patch = jnp.zeros((slots, sub), F32)
            for n, enc_ref in enumerate(enc_refs):
                patch = patch + dot(
                    mixed_ref[:, n * piece : (n + 1) * piece], enc_ref[:, pl.ds(lane, sub)]
                )
            rows_ref[j * slots : (j + 1) * slots, :] = patch.astype(BF)

    table = jnp.concatenate([table, lane_index.astype(jnp.int32)[None]])
    width = lifted.shape[1]
    return call_on_blocks(
        body,
        table,
        [lifted] + mixed + enc_pieces,
        [
            jax.ShapeDtypeStruct((rows, total_rows), F32),
            jax.ShapeDtypeStruct((rows, total_rows), BF),
            jax.ShapeDtypeStruct((size * slots, sub), BF),
        ],
        [pltpu.VMEM((3 * rows, size * slots), BF), pltpu.VMEM((size * slots, total_rows), BF)],
        2 * size * slots * (rows * (width + 3 * total_rows) + width * sub),
        2 * (size * slots * width + 3 * rows * total_rows),
    )


def unpack_home(parts, rows_own, table, slots):
    count = len(parts)
    size = table.shape[0] // 2
    total_rows, sub = parts[0].shape
    extra = [] if rows_own is None else [rows_own]

    def body(table_ref, *refs):
        total = refs[0][...].astype(F32)
        for ref in refs[1:count]:
            total = total + ref[...].astype(F32)
        total = total.astype(BF)
        slot = lax.broadcasted_iota(jnp.int32, (slots, total_rows), 0)
        gap = lax.broadcasted_iota(jnp.int32, (slots, total_rows), 1) - slot
        outs = refs[count + len(extra) :]
        for j in range(size):
            live = slot < table_ref[size + j]
            spread = jnp.where((gap == table_ref[j]) & live, 1.0, 0.0).astype(BF)
            home = dot(spread, total)
            if extra:
                own = refs[count][j * slots : (j + 1) * slots, :].astype(F32)
                home = home + jnp.where(live[:, :sub], own, 0.0)
            outs[j // 2][j % 2] = home.astype(BF)

    out = jax.ShapeDtypeStruct((2, slots, sub), BF)
    return call_on_blocks(
        body,
        table,
        parts + extra,
        [out] * (size // 2),
        [],
        2 * size * slots * total_rows * sub,
        2 * (count * total_rows + 2 * size * slots) * sub,
    )


def keys_values(mine, other, weights, lanes):
    chips = len(mine)
    _, slots, sub = mine[0].shape
    width = weights[0].shape[2]

    def body(place_ref, *refs):
        mine_refs, other_refs, weight_refs = refs[:chips], refs[chips : 2 * chips], refs[2 * chips : 4 * chips]
        out_refs = refs[4 * chips :]
        for k, out_ref in enumerate(out_refs):
            total = jnp.zeros((slots, width), F32)
            for j, weight_ref in enumerate(weight_refs):
                ref = (mine_refs, other_refs)[j % 2][j // 2]
                total = total + dot(ref[j % 2], weight_ref[k])
            out_ref[...] = total.astype(BF)

    return call_on_blocks(
        body,
        jnp.zeros((1,), jnp.int32),
        mine + other + weights,
        [jax.ShapeDtypeStruct((slots, width), BF)] * lanes,
        [],
        4 * chips * slots * sub * lanes * width,
        4 * chips * sub * lanes * width,
    )


def sort_grad(mine, other, lanes, lane_index):
    chips = len(mine)
    _, slots, sub = mine[0].shape
    per_lane = 2 * chips // lanes

    def body(place_ref, *refs):
        mine_refs, other_refs = refs[:chips], refs[chips : 2 * chips]
        for k, out_ref in enumerate(refs[2 * chips :]):
            for p in range(per_lane):
                place = ((place_ref[1] ^ k) * per_lane + p) ^ place_ref[0]
                value = mine_refs[0][0]
                for j in range(1, 2 * chips):
                    block = (mine_refs, other_refs)[j % 2][j // 2][j % 2]
                    value = jnp.where(place == j, block, value)
                out_ref[p] = value

    place = jnp.stack([lax.axis_index("seq"), lane_index]).astype(jnp.int32)
    out = jax.ShapeDtypeStruct((per_lane, slots, sub), BF)
    return call_on_blocks(body, place, mine + other, [out] * lanes, [], 0, 8 * chips * slots * sub)


def finish_grad(cot, got, count, lane_index):
    lanes = len(got)
    per_lane, slots, sub = got[0].shape

    def body(place_ref, cot_ref, *refs):
        live = lax.broadcasted_iota(jnp.int32, (slots, sub), 0) < place_ref[1]
        for k in range(lanes):
            for p in range(per_lane):
                columns = pl.ds(pl.multiple_of((p * lanes + (place_ref[0] ^ k)) * sub, sub), sub)
                total = cot_ref[:, columns].astype(F32) + refs[k][p].astype(F32)
                refs[lanes][:, columns] = jnp.where(live, total, 0.0).astype(BF)

    place = jnp.stack([lane_index, count]).astype(jnp.int32)
    return call_on_blocks(
        body, place, [cot] + got, [jax.ShapeDtypeStruct(cot.shape, BF)], [], 0, 6 * cot.size
    )[0]


def mix_pieces(pieces, weight_t, lane_index):
    size = len(pieces)
    lanes = lax.axis_size("mp")
    rows, total_rows = pieces[0].shape
    width = weight_t.shape[1]
    sub = width // lanes
    step = 256 if total_rows % 256 == 0 else total_rows

    def body(place_ref, weight_ref, *refs):
        piece_refs, out_refs, acc_ref = refs[:size], refs[size:-1], refs[-1]
        total = None
        for j, piece_ref in enumerate(piece_refs):
            start = pl.multiple_of((place_ref[0] ^ j) * rows, 16)
            part = contract_first(piece_ref[...], weight_ref[pl.ds(start, rows), :])
            total = part if total is None else total + part
        acc_ref[...] = total
        for k, out_ref in enumerate(out_refs):
            start = pl.multiple_of((place_ref[1] ^ k) * sub, sub)
            out_ref[...] = acc_ref[:, pl.ds(start, sub)].astype(BF)

    place = jnp.stack([lax.axis_index("seq"), lane_index]).astype(jnp.int32)
    spec = pltpu.PrefetchScalarGridSpec(
        num_scalar_prefetch=1,
        grid=(total_rows // step,),
        in_specs=[pl.BlockSpec(weight_t.shape, lambda r, place: (0, 0))]
        + [pl.BlockSpec((rows, step), lambda r, place: (0, r))] * size,
        out_specs=[pl.BlockSpec((step, sub), lambda r, place: (r, 0))] * lanes,
        scratch_shapes=[pltpu.VMEM((step, width), F32)],
    )
    return pl.pallas_call(
        body,
        grid_spec=spec,
        out_shape=[jax.ShapeDtypeStruct((total_rows, sub), BF)] * lanes,
        compiler_params=pltpu.CompilerParams(vmem_limit_bytes=32 * 1024 * 1024),
        cost_estimate=pl.CostEstimate(
            flops=2 * size * rows * total_rows * width,
            bytes_accessed=2 * (size * rows * (total_rows + width) + total_rows * width),
            transcendentals=0,
        ),
    )(place, weight_t, *pieces)


def outer_pieces(cot_lanes, pieces, lane_index, scale):
    size = len(pieces)
    lanes = len(cot_lanes)
    rows, total_rows = pieces[0].shape
    sub = cot_lanes[0].shape[1]
    full = size * rows
    step = block_rows(full, 256) if full % 256 else 256

    def body(place_ref, *refs):
        cot_refs, piece_refs = refs[:lanes], refs[lanes : lanes + size]
        out_ref, acc_ref = refs[lanes + size :]
        for j, piece_ref in enumerate(piece_refs):
            start = pl.multiple_of((place_ref[0] ^ j) * rows, 16)
            left = piece_ref[...]
            for k, cot_ref in enumerate(cot_refs):
                acc_ref[pl.ds(start, rows), k * sub : (k + 1) * sub] = dot(left, cot_ref[...]) * scale
        for k in range(lanes):
            top = pl.multiple_of((place_ref[1] ^ k) * sub, sub)
            for n in range(full // step):
                block = acc_ref[n * step : (n + 1) * step, k * sub : (k + 1) * sub]
                out_ref[pl.ds(top, sub), n * step : (n + 1) * step] = block.T.astype(BF)

    place = jnp.stack([lax.axis_index("seq"), lane_index]).astype(jnp.int32)
    return call_on_blocks(
        body,
        place,
        cot_lanes + pieces,
        [jax.ShapeDtypeStruct((lanes * sub, full), BF)],
        [pltpu.VMEM((full, lanes * sub), F32)],
        2 * full * total_rows * lanes * sub,
        2 * (full * total_rows + total_rows * lanes * sub + full * lanes * sub),
    )[0]


def per_device(
    byte_states,
    patch_starts,
    patch_counts,
    patch_owner,
    enc_query,
    enc_key,
    enc_value,
    enc_out,
    up_proj,
    down_proj,
    dec_query,
    dec_key,
    dec_value,
    dec_out,
    latent_cotangent,
):
    groups = lax.axis_size("seq")
    chips = groups // 2
    lanes = lax.axis_size("mp")
    here = lax.axis_index("seq")
    lane_index = lax.axis_index("mp")
    byte_count = byte_states.shape[0]
    slots = patch_starts.shape[1]
    total_rows = groups * CAP
    slice_width = up_proj.shape[0]
    sub = slice_width // lanes
    per_lane = groups // lanes
    patch_start = patch_starts[0]
    patch_total = patch_counts[0, 0]
    hidden_rows = up_proj.shape[1] // groups
    tiled = hidden_rows % 16 == 0 and sub % 128 == 0 and slots % 64 == 0 and groups <= 8
    scale = 1.0 / math.sqrt(total_rows)
    relative = jnp.arange(groups, dtype=jnp.int32) ^ here
    slot_ids = jnp.arange(slots, dtype=jnp.int32)
    positions = jnp.arange(byte_count, dtype=jnp.int32)

    enc_own = lax.dynamic_slice_in_dim(enc_out, here * slice_width, slice_width, 1)
    enc_pieces = gather_mp(enc_own)

    def cot_piece(k):
        return jnp.stack(
            [
                lax.dynamic_slice_in_dim(
                    latent_cotangent, (p * lanes + (lane_index ^ k)) * sub, sub, 1
                )
                for p in range(per_lane)
            ]
        )

    cot_got = exchange_mp([cot_piece(k) for k in range(lanes)])

    patch_end = jnp.concatenate([patch_start[1:], jnp.full((1,), byte_count, jnp.int32)])
    member = (positions[None, :] >= patch_start[:, None]) & (
        positions[None, :] < patch_end[:, None]
    )
    lengths = jnp.sum(member.astype(F32), axis=1)
    pooled = dot(member.astype(BF), byte_states)
    pooled = (pooled / jnp.maximum(lengths, 1.0)[:, None]).astype(BF)
    queries = dot(pooled, enc_query).astype(BF)
    keys_in = dot(byte_states, enc_key).astype(BF)
    values_in = dot(byte_states, enc_value).astype(BF)

    if tiled:
        up_t = up_proj.T
        keys_in, values_in, up_later = lax.optimization_barrier((keys_in, values_in, up_t))
        lifted_parts = partial_blocks(up_later, enc_pieces)
        cot_sent = sort_cot(cot_got, patch_total, lane_index)
        cot_mine, cot_other = exchange_pieces(cot_sent)
        cot_packed, table = pack_cot(cot_mine, cot_other, total_rows)
    else:
        enc_slice = jnp.concatenate(enc_pieces, axis=0)
        lifted_part = lax.dot_general(
            up_proj, enc_slice, (((0,), (1,)), ((), ())), preferred_element_type=F32
        ).astype(BF)
        lifted = scatter_sum_seq(lifted_part).astype(BF)
        cot_sent = jnp.full((groups, slots + 16, sub), patch_total.astype(F32).astype(BF))
        for k in range(lanes):
            for p in range(per_lane):
                place = ((lane_index ^ k) * per_lane + p) ^ here
                cot_sent = lax.dynamic_update_slice(cot_sent, cot_got[k][p][None], (place, 0, 0))
        cot_here = exchange_seq(cot_sent.reshape(chips, 2, slots + 16, sub)).reshape(
            groups, slots + 16, sub
        )
        counts = cot_here[:, slots, 0].astype(F32).astype(jnp.int32)
        before = relative[None, :] < relative[:, None]
        offsets = jnp.sum(jnp.where(before, counts[None, :], 0), axis=1)
        places = jnp.where(
            slot_ids[None, :] < counts[:, None], offsets[:, None] + slot_ids[None, :], -1
        ).reshape(groups * slots)
        row_ids = jnp.arange(total_rows, dtype=jnp.int32)
        selector = (row_ids[:, None] == places[None, :]).astype(BF)
        cot_packed = dot(selector, cot_here[:, :slots].reshape(groups * slots, sub)).astype(BF)

    cot_all = gather_mp(cot_packed)
    if not tiled:
        cot_slice = jnp.zeros((total_rows, slice_width), BF)
        for k in range(lanes):
            cot_slice = lax.dynamic_update_slice_in_dim(
                cot_slice, cot_all[k], (lane_index ^ k) * sub, 1
            )

    if tiled:
        queries, *lifted_parts = lax.optimization_barrier((queries, *lifted_parts))
    mixed = attend(queries, keys_in, values_in, member, enc_query.shape[1] // HD)
    if tiled:
        lifted = scatter_blocks(*lifted_parts).astype(BF)
    mixed = jnp.concatenate(gather_mp(mixed), axis=1)
    mixed_pieces = gather_seq(mixed)

    def sum_parts(got):
        total = got[0].astype(F32)
        for piece in got[1:]:
            total = total + piece.astype(F32)
        return total

    rows_of = lambda weight, k: lax.dynamic_slice_in_dim(
        weight, here * slice_width + (lane_index ^ k) * sub, sub, 0
    )
    head_pieces = exchange_mp(
        [
            jnp.concatenate([rows_of(dec_key, k), rows_of(dec_value, k)], axis=1)
            for k in range(lanes)
        ]
    )
    head_weights = jnp.stack(head_pieces)
    head_weights = gather_seq(head_weights)

    if tiled:
        hidden_pre, hidden, rows_own = hidden_kernel(
            lifted, mixed_pieces, enc_pieces, table, lane_index, total_rows, sub
        )
        hidden_pieces = gather_seq(hidden)
        down_later, _ = lax.optimization_barrier((down_proj, cot_packed))
        down_t = down_later.T
        forward_blocks = mix_pieces(hidden_pieces, down_t, lane_index)
        forward_got = exchange_mp(forward_blocks)
        down_grad = outer_pieces(cot_all, hidden_pieces, lane_index, scale)
        backward_parts = partial_blocks(down_t, cot_all, lane_index)
        backward = scatter_blocks(*backward_parts)
        inner = gelu_back(hidden_pre, backward).astype(BF)
        inner_pieces = gather_seq(inner)
        backward_blocks = mix_pieces(inner_pieces, up_t, lane_index)
        backward_got = exchange_mp(backward_blocks)
        latent_sent = unpack_home(forward_got, rows_own, table, slots)
        latent_mine, latent_other = exchange_pieces(latent_sent)
        terms = keys_values(latent_mine, latent_other, head_weights, lanes)
    else:
        mixed_all = jnp.concatenate(mixed_pieces, axis=0)
        slot_pre = contract_last(lifted, mixed_all)
        slot_hidden = jax.nn.gelu(slot_pre).astype(BF)
        hidden = contract_last(slot_hidden, selector).astype(BF)
        hidden_all = place_rows(gather_seq(hidden))
        forward_part = lax.dot_general(
            hidden_all, down_proj, (((0,), (1,)), ((), ())), preferred_element_type=F32
        ).astype(BF)
        pre_high = slot_pre.astype(BF)
        pre_low = (slot_pre - pre_high.astype(F32)).astype(BF)
        hidden_pre = contract_last(pre_high, selector) + contract_last(pre_low, selector)
        backward_partial = lax.dot_general(
            down_proj, cot_slice, (((0,), (1,)), ((), ())), preferred_element_type=F32
        ).astype(BF)
        backward = scatter_sum_seq(backward_partial)
        inner = gelu_back(hidden_pre, backward).astype(BF)
        inner_all = place_rows(gather_seq(inner))
        backward_part = lax.dot_general(
            inner_all, up_proj, (((0,), (1,)), ((), ())), preferred_element_type=F32
        ).astype(BF)
        down_grad = lax.dot_general(
            cot_slice, hidden_all, (((0,), (1,)), ((), ())), preferred_element_type=F32
        )
        down_grad = (down_grad * scale).astype(BF)

        def sum_lanes(part):
            blocks = [
                lax.dynamic_slice_in_dim(part, (lane_index ^ k) * sub, sub, 1) for k in range(lanes)
            ]
            return sum_parts(exchange_mp(blocks)).astype(BF)

        def send_home(home):
            return exchange_seq(home.astype(BF).reshape(chips, 2, slots, sub)).reshape(
                groups, slots, sub
            )

        enc_sub = lax.dynamic_slice_in_dim(enc_slice, lane_index * sub, sub, 1)
        rows_own = jnp.where((places >= 0)[:, None], dot(mixed_all, enc_sub), 0.0)
        latent_here = send_home(contract_first(selector, sum_lanes(forward_part)) + rows_own)
        terms = []
        for k in range(lanes):
            term = sum(dot(latent_here[j], head_weights[j][k]) for j in range(groups))
            terms.append(term.astype(BF))

    terms = exchange_mp(terms)
    both = sum_parts(terms).astype(BF)
    dec_queries = dot(byte_states, dec_query).astype(BF)
    dec_keys = both[:, : dec_key.shape[1]]
    dec_values = both[:, dec_key.shape[1] :]
    home_patch = (
        jnp.sum((patch_start[None, :] <= positions[:, None]).astype(jnp.int32), axis=1) - 1
    )
    allowed = slot_ids[None, :] <= home_patch[:, None]
    byte_mixed = attend(dec_queries, dec_keys, dec_values, allowed, dec_query.shape[1] // HD)
    decoded_part = dot(byte_mixed, dec_out).astype(BF)
    width_here = decoded_part.shape[1] // lanes
    got = exchange_mp(
        [
            lax.dynamic_slice_in_dim(decoded_part, (lane_index ^ k) * width_here, width_here, 1)
            for k in range(lanes)
        ]
    )
    own_cols = lax.dynamic_slice_in_dim(byte_states, lane_index * width_here, width_here, 1)
    decoded = (own_cols.astype(F32) + sum_parts(got)).astype(BF)

    if tiled:
        grad_sent = unpack_home(backward_got, None, table, slots)
        grad_mine, grad_other = exchange_pieces(grad_sent)
        grad_out = sort_grad(grad_mine, grad_other, lanes, lane_index)
        grad_got = exchange_mp(grad_out)
        patch_grad = finish_grad(latent_cotangent, grad_got, patch_total, lane_index)
        return (decoded, patch_grad, down_grad)

    grad_here = send_home(contract_first(selector, sum_lanes(backward_part)))

    def grad_piece(k):
        return jnp.stack(
            [
                lax.dynamic_index_in_dim(
                    grad_here, ((lane_index ^ k) * per_lane + p) ^ here, 0, keepdims=False
                )
                for p in range(per_lane)
            ]
        )

    grad_got = exchange_mp([grad_piece(k) for k in range(lanes)])
    grad_cols = jnp.zeros((slots, lanes * per_lane * sub), BF)
    for k in range(lanes):
        for p in range(per_lane):
            grad_cols = lax.dynamic_update_slice_in_dim(
                grad_cols, grad_got[k][p], (p * lanes + (lane_index ^ k)) * sub, 1
            )
    live = patch_owner[0] >= 0
    patch_grad = latent_cotangent.astype(F32) + grad_cols.astype(F32)
    patch_grad = jnp.where(live[:, None], patch_grad, 0.0).astype(BF)
    return (decoded, patch_grad, down_grad)


def solution(mesh):
    return jax.shard_map(
        per_device,
        mesh=mesh,
        in_specs=(
            P("seq", None),
            P("seq", None),
            P("seq", None),
            P("seq", None),
            P(None, "mp"),
            P(None, "mp"),
            P(None, "mp"),
            P("mp", None),
            P("seq", "mp"),
            P("seq", "mp"),
            P(None, "mp"),
            P(None, "mp"),
            P(None, "mp"),
            P("mp", None),
            P("seq", "mp"),
        ),
        out_specs=(P("seq", "mp"), P("seq", "mp"), P("seq", "mp")),
        check_vma=False,
    )
```

```python
import math

import jax
import jax.numpy as jnp
from jax import lax
from jax.experimental import pallas as pl
from jax.experimental.pallas import tpu as pltpu
from jax.sharding import PartitionSpec as P

HD = 64
CAP = 128
MASKED = -1e30


BF = jnp.bfloat16
F32 = jnp.float32


def gelu_back(hidden_pre, incoming):
    return jax.vjp(jax.nn.gelu, hidden_pre)[1](incoming)[0]


def attend(queries, keys_in, values_in, allowed, head_count):
    row_count = queries.shape[0]
    col_count = keys_in.shape[0]
    head_width = queries.shape[1] // head_count
    query_heads = queries.reshape(row_count, head_count, head_width)
    key_heads = keys_in.reshape(col_count, head_count, head_width)
    value_heads = values_in.reshape(col_count, head_count, head_width)
    scores = (
        jnp.einsum("rhd,chd->hrc", query_heads, key_heads, preferred_element_type=F32)
        / head_width**0.5
    )
    scores = jnp.where(allowed[None], scores, MASKED)
    weights = jax.nn.softmax(scores, axis=-1).astype(BF)
    mixed = jnp.einsum("hrc,chd->rhd", weights, value_heads, preferred_element_type=F32)
    return mixed.reshape(row_count, head_count * head_width).astype(BF)


def dot(left, right):
    return jnp.dot(left, right, preferred_element_type=F32)


def contract_last(left, right):
    return lax.dot_general(left, right, (((1,), (1,)), ((), ())), preferred_element_type=F32)


def contract_first(left, right):
    return lax.dot_general(left, right, (((0,), (0,)), ((), ())), preferred_element_type=F32)


def seq_swap(value, bits):
    return lax.ppermute(value, "seq", [(i, i ^ bits) for i in range(lax.axis_size("seq"))])


def mp_swap(value, bits):
    return lax.ppermute(value, "mp", [(i, i ^ bits) for i in range(lax.axis_size("mp"))])


def gather_mp(value):
    return [value] + [mp_swap(value, k) for k in range(1, lax.axis_size("mp"))]


def exchange_mp(pieces):
    return [pieces[0]] + [mp_swap(pieces[k], k) for k in range(1, len(pieces))]


def gather_seq(value):
    out = []
    for chip in range(lax.axis_size("seq") // 2):
        same = value if chip == 0 else seq_swap(value, 2 * chip)
        out += [same, seq_swap(same, 1)]
    return out


def exchange_seq(blocks):
    chips = blocks.shape[0]
    got = [blocks[0]] + [seq_swap(blocks[i], 2 * i) for i in range(1, chips)]
    mine = jnp.stack([piece[0] for piece in got])
    other = seq_swap(jnp.stack([piece[1] for piece in got]), 1)
    return jnp.stack([mine, other], axis=1)


def scatter_sum_seq(partial):
    size = lax.axis_size("seq")
    here = lax.axis_index("seq")
    rows = partial.shape[0] // size

    def block(j):
        return lax.dynamic_slice_in_dim(partial, (here ^ j) * rows, rows, 0)

    total = None
    for chip in list(range(1, size // 2)) + [0]:
        arrived = seq_swap(block(2 * chip + 1), 1)
        summed = block(2 * chip).astype(F32) + arrived.astype(F32)
        if chip:
            summed = seq_swap(summed.astype(BF), 2 * chip).astype(F32)
        total = summed if total is None else total + summed
    return total


def place_rows(blocks):
    here = lax.axis_index("seq")
    rows = blocks[0].shape[0]
    out = jnp.zeros((rows * len(blocks), blocks[0].shape[1]), blocks[0].dtype)
    for j, block in enumerate(blocks):
        out = lax.dynamic_update_slice_in_dim(out, block, (here ^ j) * rows, 0)
    return out


def call_on_blocks(body, scalars, operands, outs, scratch, flops, moved):
    whole = pl.BlockSpec(memory_space=pltpu.VMEM)
    return pl.pallas_call(
        body,
        out_shape=outs,
        in_specs=[pl.BlockSpec(memory_space=pltpu.SMEM)] + [whole] * len(operands),
        out_specs=[whole] * len(outs),
        scratch_shapes=scratch,
        compiler_params=pltpu.CompilerParams(vmem_limit_bytes=48 * 1024 * 1024),
        cost_estimate=pl.CostEstimate(flops=flops, bytes_accessed=moved, transcendentals=0),
    )(scalars, *operands)


def block_rows(total, most):
    best = total
    for step in range(16, most + 1, 16):
        if total % step == 0:
            best = step
    return best


def partial_blocks(weight_t, wide, lane_index=None):
    size = lax.axis_size("seq")
    rows = weight_t.shape[0] // size
    depth = weight_t.shape[1]
    chips = size // 2
    piece_rows, sub = wide[0].shape
    by_columns = lane_index is not None
    width = piece_rows if by_columns else piece_rows * len(wide)

    def body(place_ref, low_ref, high_ref, *refs):
        count = len(wide)
        wide_refs, mine_ref, other_ref = refs[:count], refs[count], refs[count + 1]
        if by_columns:
            right_ref = refs[count + 2]

            @pl.when(pl.program_id(0) == 0)
            def _():
                for k, wide_ref in enumerate(wide_refs):
                    start = pl.multiple_of((place_ref[1] ^ k) * sub, sub)
                    right_ref[:, pl.ds(start, sub)] = wide_ref[...]

            wide_refs = [right_ref]
        for left_ref, out_ref in ((low_ref, mine_ref), (high_ref, other_ref)):
            left = left_ref[...]
            for n, wide_ref in enumerate(wide_refs):
                out_ref[0, :, n * piece_rows : (n + 1) * piece_rows] = contract_last(
                    left, wide_ref[...]
                ).astype(BF)

    lane = lane_index if by_columns else lax.axis_index("mp")
    place = jnp.stack([lax.axis_index("seq"), lane]).astype(jnp.int32)
    spec = pltpu.PrefetchScalarGridSpec(
        num_scalar_prefetch=1,
        grid=(chips,),
        in_specs=[
            pl.BlockSpec((rows, depth), lambda i, place: (place[0] ^ (2 * i), 0)),
            pl.BlockSpec((rows, depth), lambda i, place: (place[0] ^ (2 * i + 1), 0)),
        ]
        + [pl.BlockSpec((piece_rows, sub), lambda i, place: (0, 0))] * len(wide),
        out_specs=[pl.BlockSpec((1, rows, width), lambda i, place: (i, 0, 0))] * 2,
        scratch_shapes=[pltpu.VMEM((width, depth), BF)] if by_columns else [],
    )
    shape = jax.ShapeDtypeStruct((chips, rows, width), BF)
    return pl.pallas_call(
        body,
        grid_spec=spec,
        out_shape=[shape, shape],
        compiler_params=pltpu.CompilerParams(vmem_limit_bytes=32 * 1024 * 1024),
        cost_estimate=pl.CostEstimate(
            flops=2 * size * rows * width * depth,
            bytes_accessed=2 * size * rows * (width + depth),
            transcendentals=0,
        ),
    )(place, weight_t, weight_t, *wide)


def add_halves(mine, other):
    chips, rows, width = mine.shape
    step = block_rows(rows, 128)

    def body(mine_ref, other_ref, *out_refs):
        for i, out_ref in enumerate(out_refs):
            total = mine_ref[i].astype(F32) + other_ref[i].astype(F32)
            out_ref[...] = total.astype(out_ref.dtype)

    whole = pl.BlockSpec((chips, step, width), lambda r: (0, r, 0))
    return pl.pallas_call(
        body,
        grid=(rows // step,),
        in_specs=[whole, whole],
        out_specs=[pl.BlockSpec((step, width), lambda r: (r, 0))] * chips,
        out_shape=[
            jax.ShapeDtypeStruct((rows, width), BF if i else F32) for i in range(chips)
        ],
        compiler_params=pltpu.CompilerParams(vmem_limit_bytes=32 * 1024 * 1024),
        cost_estimate=pl.CostEstimate(
            flops=mine.size, bytes_accessed=8 * mine.size, transcendentals=0
        ),
    )(mine, other)


def scatter_blocks(mine, other):
    arrived = seq_swap(other, 1)
    summed = add_halves(mine, arrived)
    got = [seq_swap(summed[i], 2 * i) for i in range(1, len(summed))]
    return [summed[0]] + got


def sum_parts(got):
    total = got[0].astype(F32)
    for piece in got[1:]:
        total = total + piece.astype(F32)
    return total


def sort_cot(got, count, lane_index):
    lanes = len(got)
    per_lane, slots, sub = got[0].shape
    chips = lanes * per_lane // 2

    def body(table_ref, *refs):
        got_refs, out_refs = refs[:lanes], refs[lanes:]
        for i, out_ref in enumerate(out_refs):
            for t in range(2):
                place = table_ref[0] ^ (2 * i + t)
                source = (place // per_lane) ^ table_ref[1]
                value = got_refs[0][place % per_lane]
                for k in range(1, lanes):
                    value = jnp.where(source == k, got_refs[k][place % per_lane], value)
                out_ref[t, :slots, :] = value
                out_ref[t, slots:, :] = jnp.full((16, sub), table_ref[2].astype(F32)).astype(BF)

    table = jnp.stack([lax.axis_index("seq"), lane_index, count]).astype(jnp.int32)
    out = jax.ShapeDtypeStruct((2, slots + 16, sub), BF)
    return call_on_blocks(body, table, got, [out] * chips, [], 0, 8 * chips * slots * sub)


def exchange_pieces(blocks):
    mine = [blocks[0]] + [seq_swap(blocks[i], 2 * i) for i in range(1, len(blocks))]
    return mine, [seq_swap(piece, 1) for piece in mine]


def pack_cot(mine, other, total_rows):
    chips = len(mine)
    size = 2 * chips
    sub = mine[0].shape[2]
    slots = mine[0].shape[1] - 16

    def body(place_ref, *refs):
        mine_refs, other_refs = refs[:chips], refs[chips:size]
        packed_ref, table_ref = refs[size:]
        blocks = [(refs_of[j // 2], j % 2) for j, refs_of in enumerate([mine_refs, other_refs] * chips)]
        counts = [ref[t, slots : slots + 1, 0:1].astype(F32) for ref, t in blocks]
        row = lax.broadcasted_iota(jnp.int32, (total_rows, slots), 0)
        slot = lax.broadcasted_iota(jnp.int32, (total_rows, slots), 1)
        gap = (row - slot).astype(F32)
        slot = slot.astype(F32)
        total = jnp.zeros((total_rows, sub), F32)
        for j, (ref, t) in enumerate(blocks):
            offset = jnp.zeros((1, 1), F32)
            for n in range(size):
                before = (place_ref[0] ^ n) < (place_ref[0] ^ j)
                offset = offset + jnp.where(before, counts[n], 0.0)
            spread = jnp.where((gap == offset) & (slot < counts[j]), 1.0, 0.0).astype(BF)
            total = total + dot(spread, ref[t, :slots, :])
            table_ref[j : j + 1, :] = jnp.broadcast_to(offset, (1, 128)).astype(jnp.int32)
            table_ref[size + j : size + j + 1, :] = jnp.broadcast_to(counts[j], (1, 128)).astype(
                jnp.int32
            )
        packed_ref[...] = total.astype(BF)

    place = lax.axis_index("seq").astype(jnp.int32)[None]
    packed, table = call_on_blocks(
        body,
        place,
        mine + other,
        [
            jax.ShapeDtypeStruct((total_rows, sub), BF),
            jax.ShapeDtypeStruct((2 * size, 128), jnp.int32),
        ],
        [],
        2 * size * slots * total_rows * sub,
        8 * size * slots * sub,
    )
    return packed, table[:, 0]


def hidden_kernel(lifted, mixed, enc_pieces, table, lane_index, total_rows, sub):
    terms = len(lifted)
    rows, width = lifted[0].shape
    slots = mixed[0].shape[0]
    size = len(mixed)
    piece = enc_pieces[0].shape[0]

    def body(table_ref, *refs):
        lifted_refs, refs = refs[:terms], refs[terms:]
        mixed_refs, enc_refs = refs[:size], refs[size : size + len(enc_pieces)]
        pre_ref, hidden_ref, rows_ref, stack_ref, spread_ref = refs[size + len(enc_pieces) :]
        lane = pl.multiple_of(table_ref[2 * size] * sub, sub)
        left = sum_parts([ref[...] for ref in lifted_refs]).astype(BF)
        slot = lax.broadcasted_iota(jnp.int32, (slots, total_rows), 0)
        gap = lax.broadcasted_iota(jnp.int32, (slots, total_rows), 1) - slot
        for j in range(size):
            spread_ref[j * slots : (j + 1) * slots, :] = jnp.where(
                (gap == table_ref[j]) & (slot < table_ref[size + j]), 1.0, 0.0
            ).astype(BF)
        for i in range(size // 2):
            slot_pre = jnp.concatenate(
                [contract_last(left, mixed_refs[2 * i + t][...]) for t in range(2)], axis=1
            )
            high = slot_pre.astype(BF)
            columns = slice(2 * i * slots, 2 * (i + 1) * slots)
            stack_ref[:rows, columns] = jax.nn.gelu(slot_pre).astype(BF)
            stack_ref[rows : 2 * rows, columns] = high
            stack_ref[2 * rows :, columns] = (slot_pre - high.astype(F32)).astype(BF)
        hidden_ref[...] = dot(stack_ref[:rows, :], spread_ref[...]).astype(BF)
        pre_ref[...] = dot(stack_ref[rows : 2 * rows, :], spread_ref[...]) + dot(
            stack_ref[2 * rows :, :], spread_ref[...]
        )
        for j, mixed_ref in enumerate(mixed_refs):
            patch = jnp.zeros((slots, sub), F32)
            for n, enc_ref in enumerate(enc_refs):
                patch = patch + dot(
                    mixed_ref[:, n * piece : (n + 1) * piece], enc_ref[:, pl.ds(lane, sub)]
                )
            rows_ref[j * slots : (j + 1) * slots, :] = patch.astype(BF)

    table = jnp.concatenate([table, lane_index.astype(jnp.int32)[None]])
    return call_on_blocks(
        body,
        table,
        lifted + mixed + enc_pieces,
        [
            jax.ShapeDtypeStruct((rows, total_rows), F32),
            jax.ShapeDtypeStruct((rows, total_rows), BF),
            jax.ShapeDtypeStruct((size * slots, sub), BF),
        ],
        [pltpu.VMEM((3 * rows, size * slots), BF), pltpu.VMEM((size * slots, total_rows), BF)],
        2 * size * slots * (rows * (width + 3 * total_rows) + width * sub),
        2 * (size * slots * width + 3 * rows * total_rows),
    )


def unpack_home(parts, rows_own, table, slots):
    count = len(parts)
    size = table.shape[0] // 2
    total_rows, sub = parts[0].shape
    extra = [] if rows_own is None else [rows_own]

    def body(table_ref, *refs):
        total = refs[0][...].astype(F32)
        for ref in refs[1:count]:
            total = total + ref[...].astype(F32)
        total = total.astype(BF)
        slot = lax.broadcasted_iota(jnp.int32, (slots, total_rows), 0)
        gap = lax.broadcasted_iota(jnp.int32, (slots, total_rows), 1) - slot
        outs = refs[count + len(extra) :]
        for j in range(size):
            live = slot < table_ref[size + j]
            spread = jnp.where((gap == table_ref[j]) & live, 1.0, 0.0).astype(BF)
            home = dot(spread, total)
            if extra:
                own = refs[count][j * slots : (j + 1) * slots, :].astype(F32)
                home = home + jnp.where(live[:, :sub], own, 0.0)
            outs[j // 2][j % 2] = home.astype(BF)

    out = jax.ShapeDtypeStruct((2, slots, sub), BF)
    return call_on_blocks(
        body,
        table,
        parts + extra,
        [out] * (size // 2),
        [],
        2 * size * slots * total_rows * sub,
        2 * (count * total_rows + 2 * size * slots) * sub,
    )


def keys_values(mine, other, weights, lanes):
    chips = len(mine)
    _, slots, sub = mine[0].shape
    width = weights[0].shape[2]

    def body(place_ref, *refs):
        mine_refs, other_refs, weight_refs = refs[:chips], refs[chips : 2 * chips], refs[2 * chips : 4 * chips]
        out_refs = refs[4 * chips :]
        for k, out_ref in enumerate(out_refs):
            total = jnp.zeros((slots, width), F32)
            for j, weight_ref in enumerate(weight_refs):
                ref = (mine_refs, other_refs)[j % 2][j // 2]
                total = total + dot(ref[j % 2], weight_ref[k])
            out_ref[...] = total.astype(BF)

    return call_on_blocks(
        body,
        jnp.zeros((1,), jnp.int32),
        mine + other + weights,
        [jax.ShapeDtypeStruct((slots, width), BF)] * lanes,
        [],
        4 * chips * slots * sub * lanes * width,
        4 * chips * sub * lanes * width,
    )


def sort_grad(mine, other, lanes, lane_index):
    chips = len(mine)
    _, slots, sub = mine[0].shape
    per_lane = 2 * chips // lanes

    def body(place_ref, *refs):
        mine_refs, other_refs = refs[:chips], refs[chips : 2 * chips]
        for k, out_ref in enumerate(refs[2 * chips :]):
            for p in range(per_lane):
                place = ((place_ref[1] ^ k) * per_lane + p) ^ place_ref[0]
                value = mine_refs[0][0]
                for j in range(1, 2 * chips):
                    block = (mine_refs, other_refs)[j % 2][j // 2][j % 2]
                    value = jnp.where(place == j, block, value)
                out_ref[p] = value

    place = jnp.stack([lax.axis_index("seq"), lane_index]).astype(jnp.int32)
    out = jax.ShapeDtypeStruct((per_lane, slots, sub), BF)
    return call_on_blocks(body, place, mine + other, [out] * lanes, [], 0, 8 * chips * slots * sub)


def finish_grad(cot, got, count, lane_index):
    lanes = len(got)
    per_lane, slots, sub = got[0].shape

    def body(place_ref, cot_ref, *refs):
        live = lax.broadcasted_iota(jnp.int32, (slots, sub), 0) < place_ref[1]
        for k in range(lanes):
            for p in range(per_lane):
                columns = pl.ds(pl.multiple_of((p * lanes + (place_ref[0] ^ k)) * sub, sub), sub)
                total = cot_ref[:, columns].astype(F32) + refs[k][p].astype(F32)
                refs[lanes][:, columns] = jnp.where(live, total, 0.0).astype(BF)

    place = jnp.stack([lane_index, count]).astype(jnp.int32)
    return call_on_blocks(
        body, place, [cot] + got, [jax.ShapeDtypeStruct(cot.shape, BF)], [], 0, 6 * cot.size
    )[0]


def mix_pieces(pieces, weight_t, lane_index):
    size = len(pieces)
    lanes = lax.axis_size("mp")
    rows, total_rows = pieces[0].shape
    width = weight_t.shape[1]
    sub = width // lanes
    step = 256 if total_rows % 256 == 0 else total_rows

    def body(place_ref, weight_ref, *refs):
        piece_refs, out_refs, acc_ref = refs[:size], refs[size:-1], refs[-1]
        total = None
        for j, piece_ref in enumerate(piece_refs):
            start = pl.multiple_of((place_ref[0] ^ j) * rows, 16)
            part = contract_first(piece_ref[...], weight_ref[pl.ds(start, rows), :])
            total = part if total is None else total + part
        acc_ref[...] = total
        for k, out_ref in enumerate(out_refs):
            start = pl.multiple_of((place_ref[1] ^ k) * sub, sub)
            out_ref[...] = acc_ref[:, pl.ds(start, sub)].astype(BF)

    place = jnp.stack([lax.axis_index("seq"), lane_index]).astype(jnp.int32)
    spec = pltpu.PrefetchScalarGridSpec(
        num_scalar_prefetch=1,
        grid=(total_rows // step,),
        in_specs=[pl.BlockSpec(weight_t.shape, lambda r, place: (0, 0))]
        + [pl.BlockSpec((rows, step), lambda r, place: (0, r))] * size,
        out_specs=[pl.BlockSpec((step, sub), lambda r, place: (r, 0))] * lanes,
        scratch_shapes=[pltpu.VMEM((step, width), F32)],
    )
    return pl.pallas_call(
        body,
        grid_spec=spec,
        out_shape=[jax.ShapeDtypeStruct((total_rows, sub), BF)] * lanes,
        compiler_params=pltpu.CompilerParams(vmem_limit_bytes=32 * 1024 * 1024),
        cost_estimate=pl.CostEstimate(
            flops=2 * size * rows * total_rows * width,
            bytes_accessed=2 * (size * rows * (total_rows + width) + total_rows * width),
            transcendentals=0,
        ),
    )(place, weight_t, *pieces)


def outer_pieces(cot_lanes, pieces, lane_index, scale):
    size = len(pieces)
    lanes = len(cot_lanes)
    rows, total_rows = pieces[0].shape
    sub = cot_lanes[0].shape[1]
    full = size * rows
    step = block_rows(full, 256) if full % 256 else 256

    def body(place_ref, *refs):
        cot_refs, piece_refs = refs[:lanes], refs[lanes : lanes + size]
        out_ref, acc_ref = refs[lanes + size :]
        for j, piece_ref in enumerate(piece_refs):
            start = pl.multiple_of((place_ref[0] ^ j) * rows, 16)
            left = piece_ref[...]
            for k, cot_ref in enumerate(cot_refs):
                acc_ref[pl.ds(start, rows), k * sub : (k + 1) * sub] = dot(left, cot_ref[...]) * scale
        for k in range(lanes):
            top = pl.multiple_of((place_ref[1] ^ k) * sub, sub)
            for n in range(full // step):
                block = acc_ref[n * step : (n + 1) * step, k * sub : (k + 1) * sub]
                out_ref[pl.ds(top, sub), n * step : (n + 1) * step] = block.T.astype(BF)

    place = jnp.stack([lax.axis_index("seq"), lane_index]).astype(jnp.int32)
    return call_on_blocks(
        body,
        place,
        cot_lanes + pieces,
        [jax.ShapeDtypeStruct((lanes * sub, full), BF)],
        [pltpu.VMEM((full, lanes * sub), F32)],
        2 * full * total_rows * lanes * sub,
        2 * (full * total_rows + total_rows * lanes * sub + full * lanes * sub),
    )[0]


def per_device(
    byte_states,
    patch_starts,
    patch_counts,
    patch_owner,
    enc_query,
    enc_key,
    enc_value,
    enc_out,
    up_proj,
    down_proj,
    dec_query,
    dec_key,
    dec_value,
    dec_out,
    latent_cotangent,
):
    groups = lax.axis_size("seq")
    chips = groups // 2
    lanes = lax.axis_size("mp")
    here = lax.axis_index("seq")
    lane_index = lax.axis_index("mp")
    byte_count = byte_states.shape[0]
    slots = patch_starts.shape[1]
    total_rows = groups * CAP
    slice_width = up_proj.shape[0]
    sub = slice_width // lanes
    per_lane = groups // lanes
    patch_start = patch_starts[0]
    patch_total = patch_counts[0, 0]
    hidden_rows = up_proj.shape[1] // groups
    tiled = hidden_rows % 16 == 0 and sub % 128 == 0 and slots % 64 == 0 and groups <= 8
    scale = 1.0 / math.sqrt(total_rows)
    relative = jnp.arange(groups, dtype=jnp.int32) ^ here
    slot_ids = jnp.arange(slots, dtype=jnp.int32)
    positions = jnp.arange(byte_count, dtype=jnp.int32)

    enc_own = lax.dynamic_slice_in_dim(enc_out, here * slice_width, slice_width, 1)
    enc_pieces = gather_mp(enc_own)

    def cot_piece(k):
        return jnp.stack(
            [
                lax.dynamic_slice_in_dim(
                    latent_cotangent, (p * lanes + (lane_index ^ k)) * sub, sub, 1
                )
                for p in range(per_lane)
            ]
        )

    cot_got = exchange_mp([cot_piece(k) for k in range(lanes)])

    patch_end = jnp.concatenate([patch_start[1:], jnp.full((1,), byte_count, jnp.int32)])
    member = (positions[None, :] >= patch_start[:, None]) & (
        positions[None, :] < patch_end[:, None]
    )
    lengths = jnp.sum(member.astype(F32), axis=1)
    pooled = dot(member.astype(BF), byte_states)
    pooled = (pooled / jnp.maximum(lengths, 1.0)[:, None]).astype(BF)
    queries = dot(pooled, enc_query).astype(BF)
    keys_in = dot(byte_states, enc_key).astype(BF)
    values_in = dot(byte_states, enc_value).astype(BF)

    if tiled:
        up_t = up_proj.T
        lifted_parts = partial_blocks(up_t, enc_pieces)
        cot_sent = sort_cot(cot_got, patch_total, lane_index)
        cot_mine, cot_other = exchange_pieces(cot_sent)
        cot_packed, table = pack_cot(cot_mine, cot_other, total_rows)
    else:
        enc_slice = jnp.concatenate(enc_pieces, axis=0)
        lifted_part = lax.dot_general(
            up_proj, enc_slice, (((0,), (1,)), ((), ())), preferred_element_type=F32
        ).astype(BF)
        lifted = scatter_sum_seq(lifted_part).astype(BF)
        cot_sent = jnp.full((groups, slots + 16, sub), patch_total.astype(F32).astype(BF))
        for k in range(lanes):
            for p in range(per_lane):
                place = ((lane_index ^ k) * per_lane + p) ^ here
                cot_sent = lax.dynamic_update_slice(cot_sent, cot_got[k][p][None], (place, 0, 0))
        cot_here = exchange_seq(cot_sent.reshape(chips, 2, slots + 16, sub)).reshape(
            groups, slots + 16, sub
        )
        counts = cot_here[:, slots, 0].astype(F32).astype(jnp.int32)
        before = relative[None, :] < relative[:, None]
        offsets = jnp.sum(jnp.where(before, counts[None, :], 0), axis=1)
        places = jnp.where(
            slot_ids[None, :] < counts[:, None], offsets[:, None] + slot_ids[None, :], -1
        ).reshape(groups * slots)
        row_ids = jnp.arange(total_rows, dtype=jnp.int32)
        selector = (row_ids[:, None] == places[None, :]).astype(BF)
        cot_packed = dot(selector, cot_here[:, :slots].reshape(groups * slots, sub)).astype(BF)

    cot_all = gather_mp(cot_packed)
    if not tiled:
        cot_slice = jnp.zeros((total_rows, slice_width), BF)
        for k in range(lanes):
            cot_slice = lax.dynamic_update_slice_in_dim(
                cot_slice, cot_all[k], (lane_index ^ k) * sub, 1
            )

    if tiled:
        queries, *lifted_parts = lax.optimization_barrier((queries, *lifted_parts))
    mixed = attend(queries, keys_in, values_in, member, enc_query.shape[1] // HD)
    if tiled:
        lifted = scatter_blocks(*lifted_parts)
    mixed = jnp.concatenate(gather_mp(mixed), axis=1)
    mixed_pieces = gather_seq(mixed)

    rows_of = lambda weight, k: lax.dynamic_slice_in_dim(
        weight, here * slice_width + (lane_index ^ k) * sub, sub, 0
    )
    head_pieces = exchange_mp(
        [
            jnp.concatenate([rows_of(dec_key, k), rows_of(dec_value, k)], axis=1)
            for k in range(lanes)
        ]
    )
    head_weights = jnp.stack(head_pieces)
    head_weights = gather_seq(head_weights)

    if tiled:
        hidden_pre, hidden, rows_own = hidden_kernel(
            lifted, mixed_pieces, enc_pieces, table, lane_index, total_rows, sub
        )
        hidden_pieces = gather_seq(hidden)
        down_later, _ = lax.optimization_barrier((down_proj, mixed[:16]))
        down_t = down_later.T
        forward_blocks = mix_pieces(hidden_pieces, down_t, lane_index)
        forward_got = exchange_mp(forward_blocks)
        down_grad = outer_pieces(cot_all, hidden_pieces, lane_index, scale)
        backward_parts = partial_blocks(down_t, cot_all, lane_index)
        backward = sum_parts(scatter_blocks(*backward_parts))
        inner = gelu_back(hidden_pre, backward).astype(BF)
        inner_pieces = gather_seq(inner)
        backward_blocks = mix_pieces(inner_pieces, up_t, lane_index)
        backward_got = exchange_mp(backward_blocks)
        latent_sent = unpack_home(forward_got, rows_own, table, slots)
        latent_mine, latent_other = exchange_pieces(latent_sent)
        terms = keys_values(latent_mine, latent_other, head_weights, lanes)
    else:
        mixed_all = jnp.concatenate(mixed_pieces, axis=0)
        slot_pre = contract_last(lifted, mixed_all)
        slot_hidden = jax.nn.gelu(slot_pre).astype(BF)
        hidden = contract_last(slot_hidden, selector).astype(BF)
        hidden_all = place_rows(gather_seq(hidden))
        forward_part = lax.dot_general(
            hidden_all, down_proj, (((0,), (1,)), ((), ())), preferred_element_type=F32
        ).astype(BF)
        pre_high = slot_pre.astype(BF)
        pre_low = (slot_pre - pre_high.astype(F32)).astype(BF)
        hidden_pre = contract_last(pre_high, selector) + contract_last(pre_low, selector)
        backward_partial = lax.dot_general(
            down_proj, cot_slice, (((0,), (1,)), ((), ())), preferred_element_type=F32
        ).astype(BF)
        backward = scatter_sum_seq(backward_partial)
        inner = gelu_back(hidden_pre, backward).astype(BF)
        inner_all = place_rows(gather_seq(inner))
        backward_part = lax.dot_general(
            inner_all, up_proj, (((0,), (1,)), ((), ())), preferred_element_type=F32
        ).astype(BF)
        down_grad = lax.dot_general(
            cot_slice, hidden_all, (((0,), (1,)), ((), ())), preferred_element_type=F32
        )
        down_grad = (down_grad * scale).astype(BF)

        def sum_lanes(part):
            blocks = [
                lax.dynamic_slice_in_dim(part, (lane_index ^ k) * sub, sub, 1) for k in range(lanes)
            ]
            return sum_parts(exchange_mp(blocks)).astype(BF)

        def send_home(home):
            return exchange_seq(home.astype(BF).reshape(chips, 2, slots, sub)).reshape(
                groups, slots, sub
            )

        enc_sub = lax.dynamic_slice_in_dim(enc_slice, lane_index * sub, sub, 1)
        rows_own = jnp.where((places >= 0)[:, None], dot(mixed_all, enc_sub), 0.0)
        latent_here = send_home(contract_first(selector, sum_lanes(forward_part)) + rows_own)
        terms = []
        for k in range(lanes):
            term = sum(dot(latent_here[j], head_weights[j][k]) for j in range(groups))
            terms.append(term.astype(BF))

    terms = exchange_mp(terms)
    both = sum_parts(terms).astype(BF)
    dec_queries = dot(byte_states, dec_query).astype(BF)
    dec_keys = both[:, : dec_key.shape[1]]
    dec_values = both[:, dec_key.shape[1] :]
    home_patch = (
        jnp.sum((patch_start[None, :] <= positions[:, None]).astype(jnp.int32), axis=1) - 1
    )
    allowed = slot_ids[None, :] <= home_patch[:, None]
    byte_mixed = attend(dec_queries, dec_keys, dec_values, allowed, dec_query.shape[1] // HD)
    decoded_part = dot(byte_mixed, dec_out).astype(BF)
    width_here = decoded_part.shape[1] // lanes
    got = exchange_mp(
        [
            lax.dynamic_slice_in_dim(decoded_part, (lane_index ^ k) * width_here, width_here, 1)
            for k in range(lanes)
        ]
    )
    own_cols = lax.dynamic_slice_in_dim(byte_states, lane_index * width_here, width_here, 1)
    decoded = (own_cols.astype(F32) + sum_parts(got)).astype(BF)

    if tiled:
        grad_sent = unpack_home(backward_got, None, table, slots)
        grad_mine, grad_other = exchange_pieces(grad_sent)
        grad_out = sort_grad(grad_mine, grad_other, lanes, lane_index)
        grad_got = exchange_mp(grad_out)
        patch_grad = finish_grad(latent_cotangent, grad_got, patch_total, lane_index)
        return (decoded, patch_grad, down_grad)

    grad_here = send_home(contract_first(selector, sum_lanes(backward_part)))

    def grad_piece(k):
        return jnp.stack(
            [
                lax.dynamic_index_in_dim(
                    grad_here, ((lane_index ^ k) * per_lane + p) ^ here, 0, keepdims=False
                )
                for p in range(per_lane)
            ]
        )

    grad_got = exchange_mp([grad_piece(k) for k in range(lanes)])
    grad_cols = jnp.zeros((slots, lanes * per_lane * sub), BF)
    for k in range(lanes):
        for p in range(per_lane):
            grad_cols = lax.dynamic_update_slice_in_dim(
                grad_cols, grad_got[k][p], (p * lanes + (lane_index ^ k)) * sub, 1
            )
    live = patch_owner[0] >= 0
    patch_grad = latent_cotangent.astype(F32) + grad_cols.astype(F32)
    patch_grad = jnp.where(live[:, None], patch_grad, 0.0).astype(BF)
    return (decoded, patch_grad, down_grad)


def solution(mesh):
    return jax.shard_map(
        per_device,
        mesh=mesh,
        in_specs=(
            P("seq", None),
            P("seq", None),
            P("seq", None),
            P("seq", None),
            P(None, "mp"),
            P(None, "mp"),
            P(None, "mp"),
            P("mp", None),
            P("seq", "mp"),
            P("seq", "mp"),
            P(None, "mp"),
            P(None, "mp"),
            P(None, "mp"),
            P("mp", None),
            P("seq", "mp"),
        ),
        out_specs=(P("seq", "mp"), P("seq", "mp"), P("seq", "mp")),
        check_vma=False,
    )
```
